256 devices in a mesh: expert: 32 (over y, x, core), dp: 8 (over z).
Axes of the slice: x: 4, y: 4, z: 8, core: 2. Of those that a mesh axis runs over, the one named last changes fastest.
Arguments:
- tokens: bfloat16 [32768, 2048], P(('expert', 'dp')), may hold values from -6 to 6
- cotangent: bfloat16 [32768, 2048], P(('expert', 'dp')), may hold values from -6 to 6
- gate_weights: float32 [32768, 8], P(('expert', 'dp')), may hold values from 0.02 to 0.5
- expert_ids: int32 [32768, 8], P(('expert', 'dp')), may hold values from 0 to 63, as said below
- copy_pick: int32 [32768, 8], P(('expert', 'dp')), may hold values from 0 to 1, as said below
- copy_expert: int32 [32], replicated, may hold values from 0 to 63, as said below
- up_weight: bfloat16 [64, 2048, 384], P('expert'), may hold values from -0.125 to 0.125
- down_weight: bfloat16 [64, 384, 2048], P('expert'), may hold values from -0.3125 to 0.3125
- copy_up: bfloat16 [32, 2048, 384], P('expert'), may hold values from -0.125 to 0.125
- copy_down: bfloat16 [32, 384, 2048], P('expert'), may hold values from -0.3125 to 0.3125
Outputs:
- layer_output: bfloat16 [32768, 2048], P(('expert', 'dp'))
- token_grad: bfloat16 [32768, 2048], P(('expert', 'dp'))
- gate_grad: float32 [32768, 8], P(('expert', 'dp'))
- up_grad: bfloat16 [64, 2048, 384], P('expert', 'dp')
- down_grad: bfloat16 [64, 384, 2048], P('expert', None, 'dp')
The draws below stay inside these ranges and needn't reach their ends.
Inputs may be any that keep to these rules, and one draw needn't show every extreme that they name: `expert_ids`: each row names 8 different experts. In the 128 rows of one device, the 2 experts of any one device are named 8 * 128 // 32 times together; the one of them that copy_expert lists is named at most 16 + 8 times and the other at most 16 - 8 + 8 // 2 times, and both bounds are reached in every block of rows. `copy_pick`: A 1 stands only where the pair's expert is listed in copy_expert. From the rows of one device at most 6 pairs go to one copy and at most 38 pairs go to one device (its own experts and its copy together). In each group of devices that share an index along dp, some device receives exactly 38 pairs from every device of the group, and the copy before it exactly 6 from each. `copy_expert`: entry c is one of the experts of device c - 1 along the expert axis (of the last device for entry 0); device o holds the experts 2 * o to 2 * o + 1.
All inputs are finite; a program needn't handle non-finite values.
Results may differ from the reference program's by a relative error of at most 0.014.
Values may be sent and summed in bfloat16 or wider, within the bound.
A program may use at most 128 MiB of HBM per device.

```python
import math
import jax
import jax.numpy as jnp
from jax import lax

WIDTH = 2048
CHOSEN = 8
HIDDEN_SIZE = 384
LOCAL_EXPERTS = 2
TOKENS_LOCAL = 128
EXPERTS = 64
COPIES = 32
REPLICAS = 8
TOKENS = 32768
MEAN_ROWS = 16
HOT_EXTRA = 8
MOVED_MOST = 6


def routing_layout(key):
    device_count = COPIES
    block_count = COPIES * REPLICAS
    token_rows = TOKENS_LOCAL
    pair_total = token_rows * CHOSEN
    layout_key = jax.random.fold_in(key, 17)
    hot_key, surplus_key, full_key, moved_key, order_key, token_key = jax.random.split(layout_key, 6)
    hot_local = jax.random.randint(hot_key, (device_count,), 0, LOCAL_EXPERTS)
    surplus_low = HOT_EXTRA - HOT_EXTRA // 2
    surplus = jax.random.randint(surplus_key, (block_count, device_count), surplus_low, HOT_EXTRA + 1)
    block_column = jnp.arange(block_count)[:, None]
    device_index = jnp.arange(device_count)[None, :]
    surplus = jnp.where(device_index == block_column % device_count, HOT_EXTRA, surplus)
    surplus = jnp.where(device_index == (block_column + 1) % device_count, surplus_low, surplus)
    full_device = jax.random.randint(full_key, (REPLICAS,), 0, device_count)
    moved_rows = jax.random.randint(moved_key, (block_count, device_count), 0, MOVED_MOST + 1)
    block_full = full_device[jnp.arange(block_count) % REPLICAS][:, None]
    moved_rows = jnp.where(device_index == block_full, 0, moved_rows)
    moved_rows = jnp.where(device_index == (block_full + device_count - 1) % device_count, MOVED_MOST, moved_rows)
    expert_index = jnp.arange(EXPERTS)
    owner_device = expert_index // LOCAL_EXPERTS
    hot_mask = expert_index % LOCAL_EXPERTS == hot_local[owner_device]
    counts = jnp.where(hot_mask[None, :], MEAN_ROWS + surplus[:, owner_device], MEAN_ROWS - surplus[:, owner_device])
    moved_expert = jnp.where(hot_mask[None, :], moved_rows[:, owner_device], 0)
    order_keys = jax.random.split(order_key, block_count)
    token_keys = jax.random.split(token_key, block_count)

    def one_block(expert_key, shuffle_key, block_counts, block_moved):
        expert_order = jax.random.permutation(expert_key, EXPERTS)
        run_lengths = block_counts[expert_order]
        run_ends = jnp.cumsum(run_lengths)
        position = jnp.arange(pair_total)
        run_index = jnp.searchsorted(run_ends, position, side='right')
        chosen_expert = expert_order[run_index]
        run_offset = position - (run_ends[run_index] - run_lengths[run_index])
        copy_flag = (run_offset < block_moved[chosen_expert]).astype(jnp.int32)
        token_order = jax.random.permutation(shuffle_key, token_rows)
        token_slot = token_order[position % token_rows]
        column_index = position // token_rows
        chosen_ids = jnp.zeros((token_rows, CHOSEN), jnp.int32).at[token_slot, column_index].set(chosen_expert.astype(jnp.int32))
        pick_table = jnp.zeros((token_rows, CHOSEN), jnp.int32).at[token_slot, column_index].set(copy_flag)
        return (chosen_ids, pick_table)
    chosen_ids, pick_table = jax.vmap(one_block)(order_keys, token_keys, counts, moved_expert)
    previous = (jnp.arange(device_count) + device_count - 1) % device_count
    copy_table = (previous * LOCAL_EXPERTS + hot_local[previous]).astype(jnp.int32)
    return (chosen_ids.reshape(block_count * token_rows, CHOSEN), pick_table.reshape(block_count * token_rows, CHOSEN), copy_table)


def draw_expert_ids(key, part):
    return routing_layout(key)[0]


def draw_copy_pick(key, part):
    return routing_layout(key)[1]


def draw_copy_expert(key, part):
    return routing_layout(key)[2]


def level_of(key, extent, shards, least, top_value):
    def one(dim, shards_of):
        steps = jax.random.uniform(jax.random.fold_in(jax.random.fold_in(key, 6), dim), (shards_of,), jnp.float32, least / len(shards), top_value / len(shards))
        return jnp.repeat(jnp.exp(steps), extent[dim] // shards_of).reshape((-1,) + (1,) * (len(extent) - dim - 1))

    factor_of = one(*shards[0])
    for cut in shards[1:]:
        factor_of = factor_of * one(*cut)
    return factor_of


def scatter_about(own_key, shape, deviation, most, shards=(), kind=jnp.bfloat16):
    values = jax.random.normal(own_key, shape, jnp.float32) * deviation
    if len(shards) > 0:
        values = level_of(own_key, shape, shards, -0.22, 0.18) * values
    return jnp.clip(values, min=-most, max=most).astype(kind)


def setup_inputs(seed: int = 0) -> dict:
    seeds = jax.random.split(jax.random.key(seed), 11)
    tokens = scatter_about(seeds[0], (TOKENS, WIDTH), 1.0, 6.0, ((0, 256),))
    cotangent = scatter_about(seeds[1], (TOKENS, WIDTH), 1.0, 6.0, ((0, 256),))
    gate_weights = jnp.clip(jnp.exp(math.log(0.5) - 3.218876 * jax.random.uniform(seeds[2], (TOKENS, CHOSEN), jnp.float32) ** level_of(seeds[2], (TOKENS, CHOSEN), ((0, 256),), -0.2, 0.2)), 0.02, 0.5)
    expert_ids = draw_expert_ids(jax.random.fold_in(seeds[10], 71), 0)
    copy_pick = draw_copy_pick(jax.random.fold_in(seeds[10], 71), 0)
    copy_expert = draw_copy_expert(jax.random.fold_in(seeds[10], 71), 0)
    up_weight = scatter_about(seeds[6], (EXPERTS, WIDTH, HIDDEN_SIZE), WIDTH ** -0.5, 0.125, ((0, 32),))
    down_weight = scatter_about(seeds[7], (EXPERTS, HIDDEN_SIZE, WIDTH), HIDDEN_SIZE ** -0.5, 0.3125, ((0, 32),))
    copy_up = scatter_about(seeds[8], (COPIES, WIDTH, HIDDEN_SIZE), WIDTH ** -0.5, 0.125, ((0, 32),))
    copy_down = scatter_about(seeds[9], (COPIES, HIDDEN_SIZE, WIDTH), HIDDEN_SIZE ** -0.5, 0.3125, ((0, 32),))
    return dict(tokens=tokens, cotangent=cotangent, gate_weights=gate_weights, expert_ids=expert_ids, copy_pick=copy_pick, copy_expert=copy_expert, up_weight=up_weight, down_weight=down_weight, copy_up=copy_up, copy_down=copy_down)


def silu_slope(values):
    sigma_values = jax.nn.sigmoid(values)
    return sigma_values * (1.0 + values * (1.0 - sigma_values))


def rounded(values):
    return lax.optimization_barrier(values.astype(jnp.bfloat16)).astype(jnp.float32)


def expert_rows(inputs, scales, cotan_rows, weight_up, weight_down):
    linear_part = jnp.dot(inputs, weight_up, preferred_element_type=jnp.float32)
    active = jax.nn.silu(linear_part).astype(jnp.bfloat16)
    outputs = jnp.dot(active, weight_down, preferred_element_type=jnp.float32).astype(jnp.bfloat16)
    scaled = (scales[:, None] * cotan_rows.astype(jnp.float32)).astype(jnp.bfloat16)
    active_grad = jnp.dot(scaled, weight_down.T, preferred_element_type=jnp.float32)
    linear_grad = (active_grad * silu_slope(linear_part)).astype(jnp.bfloat16)
    pair_grad = jnp.dot(linear_grad, weight_up.T, preferred_element_type=jnp.float32).astype(jnp.bfloat16)
    up_part = jnp.dot(inputs.T, linear_grad, preferred_element_type=jnp.float32)
    down_part = jnp.dot(active.T, scaled, preferred_element_type=jnp.float32)
    return outputs, pair_grad, up_part, down_part


def reference(tokens, cotangent, gate_weights, expert_ids, copy_pick, copy_expert, up_weight, down_weight, copy_up, copy_down):
    group_size = COPIES * TOKENS_LOCAL
    pair_total = group_size * CHOSEN
    primary_most = COPIES * (MEAN_ROWS + HOT_EXTRA)
    copy_most = COPIES * MOVED_MOST

    def regroup(values):
        shaped = values.reshape((COPIES, REPLICAS, TOKENS_LOCAL) + values.shape[1:])
        return jnp.swapaxes(shaped, 0, 1).reshape((REPLICAS, group_size) + values.shape[1:])

    def ungroup(values):
        shaped = values.reshape((REPLICAS, COPIES, TOKENS_LOCAL) + values.shape[2:])
        return jnp.swapaxes(shaped, 0, 1).reshape((TOKENS,) + values.shape[2:])

    def one_group(totals, members):
        up_total, down_total = totals
        group_rows, group_cotan, group_gates, group_ids, group_picks = members
        flat_gates = group_gates.reshape(pair_total)
        flat_ids = group_ids.reshape(pair_total)
        flat_picks = group_picks.reshape(pair_total)

        def serve(carried, selected, most, weight_up, weight_down):
            mixed_sum, grad_sum, gate_grads = carried
            pair_index = jnp.nonzero(selected, size=most, fill_value=pair_total)[0].astype(jnp.int32)
            present = pair_index < pair_total
            clipped = jnp.minimum(pair_index, pair_total - 1)
            row_index = clipped // CHOSEN
            target_row = pair_index // CHOSEN
            inputs = jnp.where(present[:, None], group_rows[row_index], jnp.zeros((), jnp.bfloat16))
            cotan_rows = jnp.where(present[:, None], group_cotan[row_index], jnp.zeros((), jnp.bfloat16))
            scales = jnp.where(present, flat_gates[clipped], jnp.zeros((), jnp.float32))
            outputs, pair_grad, up_part, down_part = expert_rows(inputs, scales, cotan_rows, weight_up, weight_down)
            wide_out = outputs.astype(jnp.float32)
            mixed_sum = mixed_sum.at[target_row].add(scales[:, None] * wide_out, mode="drop")
            grad_sum = grad_sum.at[target_row].add(pair_grad.astype(jnp.float32), mode="drop")
            gate_grads = gate_grads.at[pair_index].set(jnp.sum(cotan_rows.astype(jnp.float32) * wide_out, axis=1), mode="drop")
            return (mixed_sum, grad_sum, gate_grads), (rounded(up_part), rounded(down_part))

        def primary(carried, expert):
            selected = (flat_ids == expert) & (flat_picks == 0)
            return serve(carried, selected, primary_most, up_weight[expert], down_weight[expert])

        def replica(carried, device):
            source = (device + COPIES - 1) % COPIES
            selected = (flat_picks == 1) & (flat_ids // LOCAL_EXPERTS == source)
            return serve(carried, selected, copy_most, copy_up[device], copy_down[device])

        initial = (jnp.zeros((group_size, WIDTH), jnp.float32), jnp.zeros((group_size, WIDTH), jnp.float32), jnp.zeros((pair_total,), jnp.float32))
        carried, (own_up, own_down) = lax.scan(primary, initial, jnp.arange(EXPERTS, dtype=jnp.int32))
        carried, (copied_up, copied_down) = lax.scan(replica, carried, jnp.arange(COPIES, dtype=jnp.int32))
        up_total = (up_total + own_up).at[copy_expert].add(copied_up)
        down_total = (down_total + own_down).at[copy_expert].add(copied_down)
        mixed_sum, grad_sum, gate_grads = carried
        return (up_total, down_total), (mixed_sum.astype(jnp.bfloat16), grad_sum.astype(jnp.bfloat16), gate_grads.reshape(group_size, CHOSEN))

    zeros_up = jnp.zeros((EXPERTS, WIDTH, HIDDEN_SIZE), jnp.float32)
    zeros_down = jnp.zeros((EXPERTS, HIDDEN_SIZE, WIDTH), jnp.float32)
    members = (regroup(tokens), regroup(cotangent), regroup(gate_weights), regroup(expert_ids), regroup(copy_pick))
    totals, (mixed_groups, grad_groups, gate_groups) = lax.scan(one_group, (zeros_up, zeros_down), members)
    return (ungroup(mixed_groups), ungroup(grad_groups), ungroup(gate_groups), totals[0].astype(jnp.bfloat16), totals[1].astype(jnp.bfloat16))
```

```python
import functools

import jax
import jax.numpy as jnp
from jax import lax
from jax.experimental import pallas as pl
from jax.experimental.pallas import tpu as pltpu
from jax.sharding import PartitionSpec as P

SIDE = 4
HOT, COLD, COPY = 24, 12, 6
SLOTS = 48
HOT_U, COLD_U, COPY_U = SIDE * HOT, SIDE * COLD, 32
UNIT = HOT_U + COLD_U + COPY_U
SPANS = ((0, HOT_U), (HOT_U, COLD_U), (HOT_U + COLD_U, COPY_U))
BF = jnp.bfloat16
F32 = jnp.float32
EXACT = lax.Precision.HIGHEST


def iota(shape, dim):
    return lax.broadcasted_iota(jnp.int32, shape, dim)


def route_kernel(ids_ref, picks_ref, gates_ref, listed_ref, table_ref, dest_ref, slot_ref):
    rows, chosen = ids_ref.shape
    ids, picks, gates = ids_ref[...], picks_ref[...], gates_ref[...]
    listed = listed_ref[...]
    devices = listed.shape[1]
    before = (iota((rows, rows), 0) > iota((rows, rows), 1)).astype(BF)
    lanes = iota((rows, 128), 1)
    token = iota((rows, 128), 0).astype(F32) + 1.0
    offset = jnp.zeros((1, 128), F32)
    table = jnp.zeros((devices, 128), F32)
    for k in range(chosen):
        e, p, g = ids[:, k : k + 1], picks[:, k : k + 1], gates[:, k : k + 1]
        hot = jnp.max((e == listed).astype(jnp.int32), axis=1, keepdims=True)
        dest = (e // 2 + p) % devices
        region = jnp.where(p == 1, 2, 1 - hot)
        hit = (region * devices + dest == lanes).astype(F32)
        ahead = jnp.dot(before, hit.astype(BF), preferred_element_type=F32) + offset
        rank = jnp.sum(hit * ahead, axis=1, keepdims=True).astype(jnp.int32)
        offset = offset + jnp.sum(hit, axis=0, keepdims=True)
        base = jnp.where(region == 0, 0, jnp.where(region == 1, HOT, HOT + COLD))
        slot = base + rank
        to = (dest == iota((rows, devices), 1)).astype(F32)
        value = jnp.where(slot == lanes, token, 0.0) + jnp.where(slot + 64 == lanes, g, 0.0)
        table = table + lax.dot_general(
            to, value, (((0,), (0,)), ((), ())), precision=EXACT, preferred_element_type=F32
        )
        dest_ref[:, k : k + 1] = dest
        slot_ref[:, k : k + 1] = slot
    table_ref[...] = table


def route(ids, picks, gates, listed):
    rows, chosen = ids.shape
    vmem = pl.BlockSpec(memory_space=pltpu.VMEM)
    return pl.pallas_call(
        route_kernel,
        out_shape=(
            jax.ShapeDtypeStruct((listed.shape[0], 128), F32),
            jax.ShapeDtypeStruct((rows, chosen), jnp.int32),
            jax.ShapeDtypeStruct((rows, chosen), jnp.int32),
        ),
        in_specs=[vmem] * 4,
        out_specs=(vmem,) * 3,
        name="route",
    )(ids, picks, gates, listed.reshape(1, -1))


def gate_kernel(dest_ref, slot_ref, back_ref, out_ref):
    rows, chosen = dest_ref.shape
    back = back_ref[...]
    devices = back.shape[0]
    for k in range(chosen):
        to = (dest_ref[:, k : k + 1] == iota((rows, devices), 1)).astype(F32)
        picked = jnp.dot(to, back, precision=EXACT, preferred_element_type=F32)
        mine = jnp.where(slot_ref[:, k : k + 1] == iota((rows, 128), 1), picked, 0.0)
        out_ref[:, k : k + 1] = jnp.sum(mine, axis=1, keepdims=True)


def gate_back(dest, slot, back):
    vmem = pl.BlockSpec(memory_space=pltpu.VMEM)
    return pl.pallas_call(
        gate_kernel,
        out_shape=jax.ShapeDtypeStruct(dest.shape, F32),
        in_specs=[vmem] * 3,
        out_specs=vmem,
        name="gate_back",
    )(dest, slot, back)


class Place:
    def __init__(self):
        me = lax.axis_index("expert")
        self.me = me
        self.core = me % 2
        x = (me // 2) % SIDE
        y = me // (2 * SIDE)
        self.s = x * (1 - self.core) + y * self.core
        self.b = y * (1 - self.core) + x * self.core

    def at(self, db, ds):
        b = (self.b + db + SIDE) % SIDE
        s = (self.s + ds + SIDE) % SIDE
        y = b * (1 - self.core) + s * self.core
        x = s * (1 - self.core) + b * self.core
        return {"expert": (y * SIDE + x) * 2 + self.core}

    def partner(self):
        return {"expert": self.me + 1 - 2 * self.core}


def greet(place):
    barrier = pltpu.get_barrier_semaphore()
    others = [place.at(0, 1), place.at(0, -1), place.at(1, 0), place.at(-1, 0), place.partner()]
    for other in others:
        pl.semaphore_signal(barrier, inc=1, device_id=other, device_id_type=pl.DeviceIdType.MESH)
    pl.semaphore_wait(barrier, len(others))


def remote(src, dst, send, recv, device):
    return pltpu.make_async_remote_copy(
        src_ref=src,
        dst_ref=dst,
        send_sem=send,
        recv_sem=recv,
        device_id=device,
        device_id_type=pl.DeviceIdType.MESH,
    )


def gather_kernel(
    tok_ref, cot_ref, pick_ref, hot_t, cold_t, copy_t, hot_c, cold_c, copy_c,
    held, rows, own_sem, send, recv, out_sem,
):
    place = Place()
    rows_of = tok_ref.shape[0]
    half = rows_of // 2
    width = tok_ref.shape[1]
    sources = (tok_ref, cot_ref)
    outs = ((hot_t, cold_t, copy_t), (hot_c, cold_c, copy_c))
    started = []
    greet(place)

    def start(copy):
        copy.start()
        started.append(copy)
        return copy

    def spot(a, db, ds, part=None):
        b = (place.b + db + SIDE) % SIDE
        s = (place.s + ds + SIDE) % SIDE
        first = pl.multiple_of(s * rows_of, rows_of)
        if part is None:
            return held.at[a, b, pl.ds(first, rows_of)]
        return held.at[a, b, pl.ds(pl.multiple_of(first + part * half, half), half)]

    def full_s(a, sign):
        return remote(
            sources[a], spot(a, 0, 0), send.at[0, 0, (1 - sign) // 2, a, 0],
            recv.at[0, 0, (1 - sign) // 2, a, 0], place.at(0, sign))

    def half_s(a, sign):
        part = (1 - sign) // 2
        return remote(
            spot(a, 0, -sign, part), spot(a, 0, -sign, part), send.at[1, 0, part, a, 0],
            recv.at[1, 0, part, a, 0], place.at(0, sign))

    def full_b(a, sign, ds):
        src = sources[a] if ds == 0 else spot(a, 0, ds)
        return remote(
            src, spot(a, 0, ds), send.at[0, 1, (1 - sign) // 2, a, ds % SIDE],
            recv.at[0, 1, (1 - sign) // 2, a, ds % SIDE], place.at(sign, 0))

    def half_b(a, sign, ds):
        part = (1 - sign) // 2
        return remote(
            spot(a, -sign, ds, part), spot(a, -sign, ds, part),
            send.at[1, 1, part, a, ds % SIDE], recv.at[1, 1, part, a, ds % SIDE],
            place.at(sign, 0))

    def pick(db):
        b = (place.b + db + SIDE) % SIDE
        slot = db % SIDE
        to = place.core * SIDE + b
        for a in range(2):

            @pl.loop(0, width // 512)
            def _(j):
                cols = pl.ds(pl.multiple_of(j * 512, 512), 512)
                rows[slot, a, :, cols] = jnp.dot(
                    pick_ref[b], held[a, b, :, cols], preferred_element_type=F32
                ).astype(BF)

            for r, (first, count) in enumerate(SPANS):
                copy = pltpu.make_async_copy(
                    rows.at[slot, a, pl.ds(first, count)], outs[a][r].at[to],
                    out_sem.at[0, slot, a, r])
                copy.start()
                kept.append(copy)
                start(
                    remote(
                        rows.at[slot, a, pl.ds(UNIT + first, count)], outs[a][r].at[to],
                        out_sem.at[1, slot, a, r], out_sem.at[2, slot, a, r],
                        place.partner()))

    kept = []
    for a in range(2):
        for sign in (1, -1):
            start(full_s(a, sign))
        for sign in (1, -1):
            start(full_b(a, sign, 0))
    for a in range(2):
        copy = pltpu.make_async_copy(sources[a], spot(a, 0, 0), own_sem.at[a])
        copy.start()
        kept.append(copy)
    for a in range(2):
        for sign in (1, -1):
            full_s(a, sign).wait_recv()
            start(half_s(a, sign))
            for way in (1, -1):
                start(full_b(a, way, -sign))
        for sign in (1, -1):
            full_b(a, sign, 0).wait_recv()
            start(half_b(a, sign, 0))
    for a in range(2):
        for sign in (1, -1):
            half_s(a, sign).wait_recv()
        for way in (1, -1):
            start(full_b(a, way, 2))
    for copy in kept:
        copy.wait()
    kept = []
    pick(0)
    for a in range(2):
        for ds in (-1, 1):
            for sign in (1, -1):
                full_b(a, sign, ds).wait_recv()
                start(half_b(a, sign, ds))
    for a in range(2):
        for sign in (1, -1):
            full_b(a, sign, 2).wait_recv()
            start(half_b(a, sign, 2))
    pick(1)
    pick(-1)
    for a in range(2):
        for ds in (0, -1, 1, 2):
            for sign in (1, -1):
                half_b(a, sign, ds).wait_recv()
    pick(2)
    for copy in kept:
        copy.wait()
    for slot in range(SIDE):
        for a in range(2):
            b = (place.b + slot) % SIDE
            to = (1 - place.core) * SIDE + b
            for r, (first, count) in enumerate(SPANS):
                remote(
                    rows.at[slot, a, pl.ds(UNIT + first, count)], outs[a][r].at[to],
                    out_sem.at[1, slot, a, r], out_sem.at[2, slot, a, r],
                    place.partner()).wait_recv()
    for copy in started:
        copy.wait_send()


def gather_rows(tokens, cotangent, picks):
    width = tokens.shape[1]
    rows_of = tokens.shape[0]
    shapes = [jax.ShapeDtypeStruct((2 * SIDE, count, width), BF) for _, count in SPANS]
    anywhere = pl.BlockSpec(memory_space=pl.ANY)
    return pl.pallas_call(
        gather_kernel,
        out_shape=tuple(shapes + shapes),
        in_specs=[anywhere, anywhere, pl.BlockSpec(memory_space=pltpu.VMEM)],
        out_specs=(anywhere,) * 6,
        scratch_shapes=[
            pltpu.VMEM((2, SIDE, SIDE * rows_of, width), BF),
            pltpu.VMEM((SIDE, 2, 2 * UNIT, width), BF),
            pltpu.SemaphoreType.DMA((2,)),
            pltpu.SemaphoreType.DMA((2, 2, 2, 2, SIDE)),
            pltpu.SemaphoreType.DMA((2, 2, 2, 2, SIDE)),
            pltpu.SemaphoreType.DMA((3, SIDE, 2, 3)),
        ],
        compiler_params=pltpu.CompilerParams(
            collective_id=0, has_side_effects=True, vmem_limit_bytes=60 << 20
        ),
        name="gather_rows",
    )(tokens, cotangent, picks)


def scatter_kernel(
    hot_o, cold_o, copy_o, hot_g, cold_g, copy_g, spread_ref, out_ref, grad_ref,
    rows, sums, first_in, second_in, third_in, fourth_in,
    in_sem, send_r, recv_r, send_1, recv_1, send_2, recv_2, send_3, recv_3, send_4, recv_4,
):
    place = Place()
    width = out_ref.shape[1]
    rows_of = out_ref.shape[0]
    half = rows_of // 2
    ins = ((hot_o, cold_o, copy_o), (hot_g, cold_g, copy_g))
    order = (2, 3, 1, 0)
    started = []
    greet(place)

    def start(copy):
        copy.start()
        started.append(copy)

    def unit_copies(slot, a, r):
        first, count = SPANS[r]
        b = (place.b + slot) % SIDE
        return pltpu.make_async_copy(
            ins[a][r].at[place.core * SIDE + b], rows.at[slot, a, pl.ds(first, count)],
            in_sem.at[slot, a, r])

    def unit_sends(slot, a, r):
        first, count = SPANS[r]
        b = (place.s + slot) % SIDE
        return remote(
            ins[a][r].at[(1 - place.core) * SIDE + b],
            rows.at[slot, a, pl.ds(UNIT + first, count)],
            send_r.at[slot, a, r], recv_r.at[slot, a, r], place.partner())

    def chunk(slot, a, ds, part=None):
        s = (place.s + ds + SIDE) % SIDE
        first = pl.multiple_of(s * rows_of, rows_of)
        if part is None:
            return sums.at[slot, a, pl.ds(first, rows_of)]
        return sums.at[slot, a, pl.ds(pl.multiple_of(first + part * half, half), half)]

    def far(slot, a, sign):
        part = (1 - sign) // 2
        return remote(
            chunk(slot, a, 2, part), first_in.at[slot, a, part],
            send_1.at[slot, a, part], recv_1.at[slot, a, part], place.at(0, sign))

    def near(slot, a, sign, part):
        way = (1 - sign) // 2
        return remote(
            chunk(slot, a, sign, part), second_in.at[slot, a, way, pl.ds(part * half, half)],
            send_2.at[slot, a, way, part], recv_2.at[slot, a, way, part],
            place.at(0, sign))

    def far_b(a, sign):
        part = (1 - sign) // 2
        return remote(
            chunk(2, a, 0, part), third_in.at[a, part],
            send_3.at[a, part], recv_3.at[a, part], place.at(sign, 0))

    def near_b(a, sign, part):
        way = (1 - sign) // 2
        return remote(
            chunk(sign % SIDE, a, 0, part), fourth_in.at[a, way, pl.ds(part * half, half)],
            send_4.at[a, way, part], recv_4.at[a, way, part], place.at(sign, 0))

    def add(into, *others):
        total = into[...].astype(F32)
        for other in others:
            total = total + other[...].astype(F32)
        into[...] = total.astype(BF)

    for slot in order:
        for a in range(2):
            for r in range(3):
                start(unit_sends(slot, a, r))
                unit_copies(slot, a, r).start()

    def expand(slot):
        b = (place.b + slot) % SIDE
        for a in range(2):
            for r in range(3):
                unit_copies(slot, a, r).wait()
                unit_sends(slot, a, r).wait_recv()

            @pl.loop(0, width // 512)
            def _(j):
                cols = pl.ds(pl.multiple_of(j * 512, 512), 512)
                sums[slot, a, :, cols] = jnp.dot(
                    spread_ref[b], rows[slot, a, :, cols], preferred_element_type=F32
                ).astype(BF)

            for sign in (1, -1):
                start(far(slot, a, sign))
            for sign in (1, -1):
                start(near(slot, a, sign, (1 + sign) // 2))

    def pass_on(slot):
        for a in range(2):
            for sign in (1, -1):
                part = (1 - sign) // 2
                far(slot, a, sign).wait_recv()
                add(chunk(slot, a, sign, part), first_in.at[slot, a, part])
                start(near(slot, a, sign, part))

    def finish(slot):
        for a in range(2):
            for sign in (1, -1):
                for part in range(2):
                    near(slot, a, sign, part).wait_recv()
            add(chunk(slot, a, 0), second_in.at[slot, a, 0], second_in.at[slot, a, 1])

    expand(2)
    expand(3)
    pass_on(2)
    expand(1)
    pass_on(3)
    finish(2)
    for a in range(2):
        for sign in (1, -1):
            start(far_b(a, sign))
    expand(0)
    pass_on(1)
    finish(3)
    for a in range(2):
        start(near_b(a, -1, 0))
    pass_on(0)
    finish(1)
    for a in range(2):
        start(near_b(a, 1, 1))
    for a in range(2):
        for sign in (1, -1):
            part = (1 - sign) // 2
            far_b(a, sign).wait_recv()
            add(chunk(sign % SIDE, a, 0, part), third_in.at[a, part])
            start(near_b(a, sign, part))
    finish(0)
    for a, result in ((0, out_ref), (1, grad_ref)):
        for sign in (1, -1):
            for part in range(2):
                near_b(a, sign, part).wait_recv()
        own = chunk(0, a, 0)
        result[...] = (
            own[...].astype(F32) + fourth_in[a, 0].astype(F32) + fourth_in[a, 1].astype(F32)
        ).astype(BF)
    for copy in started:
        copy.wait_send()


def scatter_rows(out_rows, grad_rows, spread, rows_of):
    width = out_rows[0].shape[-1]
    half = rows_of // 2
    anywhere = pl.BlockSpec(memory_space=pl.ANY)
    vmem = pl.BlockSpec(memory_space=pltpu.VMEM)
    shape = jax.ShapeDtypeStruct((rows_of, width), BF)
    dma = pltpu.SemaphoreType.DMA
    return pl.pallas_call(
        scatter_kernel,
        out_shape=(shape, shape),
        in_specs=[anywhere] * 6 + [vmem],
        out_specs=(vmem, vmem),
        scratch_shapes=[
            pltpu.VMEM((SIDE, 2, 2 * UNIT, width), BF),
            pltpu.VMEM((SIDE, 2, SIDE * rows_of, width), BF),
            pltpu.VMEM((SIDE, 2, 2, half, width), BF),
            pltpu.VMEM((SIDE, 2, 2, rows_of, width), BF),
            pltpu.VMEM((2, 2, half, width), BF),
            pltpu.VMEM((2, 2, rows_of, width), BF),
            dma((SIDE, 2, 3)),
            dma((SIDE, 2, 3)),
            dma((SIDE, 2, 3)),
            dma((SIDE, 2, 2)),
            dma((SIDE, 2, 2)),
            dma((SIDE, 2, 2, 2)),
            dma((SIDE, 2, 2, 2)),
            dma((2, 2)),
            dma((2, 2)),
            dma((2, 2, 2)),
            dma((2, 2, 2)),
        ],
        compiler_params=pltpu.CompilerParams(
            collective_id=1, has_side_effects=True, vmem_limit_bytes=62 << 20
        ),
        name="scatter_rows",
    )(*out_rows, *grad_rows, spread)


def regions(values, fill):
    lead = values.shape[:-2]
    hot = values[..., :HOT].reshape(*lead, HOT_U)
    cold = values[..., HOT : HOT + COLD].reshape(*lead, COLD_U)
    copied = values[..., HOT + COLD : HOT + COLD + COPY].reshape(*lead, SIDE * COPY)
    pad = [(0, 0)] * len(lead) + [(0, COPY_U - SIDE * COPY)]
    return hot, cold, jnp.pad(copied, pad, constant_values=fill)


def local(
    tokens,
    cotangent,
    gate_weights,
    expert_ids,
    copy_pick,
    copy_expert,
    up_weight,
    down_weight,
    copy_up,
    copy_down,
):
    devices = lax.axis_size("expert")
    me = lax.axis_index("expert")
    core = me % 2
    rows_of, width = tokens.shape
    table, dest, slot = route(expert_ids, copy_pick, gate_weights, copy_expert)
    sent = jnp.broadcast_to(
        table.reshape(devices // 2, 1, 2, 128), (devices // 2, 2, 2, 128)
    ).reshape(devices, 2, 128)
    tables = lax.all_to_all(sent, "expert", split_axis=0, concat_axis=0, tiled=True)
    grid = tables.reshape(SIDE, SIDE, 2, 2, 128)
    by_unit = jnp.stack([grid[:, :, 0], jnp.swapaxes(grid[:, :, 1], 0, 1)])
    mine = jnp.where(core == 0, by_unit[:, :, :, 0], by_unit[:, :, :, 1])
    gates = regions(mine[..., 64 : 64 + SLOTS], 0.0)
    named = jnp.where(core == 0, by_unit[0], by_unit[1])[..., :SLOTS].astype(jnp.int32)
    named = jnp.where(core == 0, named, named[:, :, ::-1])
    place = jnp.arange(SIDE, dtype=jnp.int32)[None, :, None, None] * rows_of
    named = jnp.where(named > 0, place + named - 1, -1)
    named = jnp.concatenate(regions(jnp.moveaxis(named, 2, 1), -1), axis=-1)
    named = named.reshape(SIDE, 2 * UNIT)
    sites = jnp.arange(SIDE * rows_of, dtype=jnp.int32)
    picks = (named[:, :, None] == sites[None, None, :]).astype(BF)
    spread = (named[:, None, :] == sites[None, :, None]).astype(BF)

    gathered = gather_rows(tokens, cotangent, picks)
    hot_slot = copy_expert[(me + 1) % devices] % 2
    region_up = [up_weight[hot_slot], up_weight[1 - hot_slot], copy_up[0]]
    region_down = [down_weight[hot_slot], down_weight[1 - hot_slot], copy_down[0]]
    out_rows, grad_rows, gate_rows, up_parts, down_parts = [], [], [], [], []
    for r, (_, count) in enumerate(SPANS):
        total = 2 * SIDE * count
        rows = gathered[r].reshape(total, width)
        cots = gathered[3 + r].reshape(total, width).astype(F32)
        scale = gates[r].reshape(total, 1)
        linear = jnp.dot(rows, region_up[r], preferred_element_type=F32)
        sigma = jax.nn.sigmoid(linear)
        active = (linear * sigma).astype(BF)
        served = jnp.dot(active, region_down[r], preferred_element_type=F32)
        gate_rows.append(jnp.sum(cots * served, axis=1))
        out_rows.append((scale * served).astype(BF).reshape(2 * SIDE, count, width))
        scaled = (scale * cots).astype(BF)
        active_grad = jnp.dot(scaled, region_down[r].T, preferred_element_type=F32)
        linear_grad = (active_grad * (sigma * (1.0 + linear * (1.0 - sigma)))).astype(BF)
        grad_rows.append(
            jnp.dot(linear_grad, region_up[r].T, preferred_element_type=F32)
            .astype(BF)
            .reshape(2 * SIDE, count, width)
        )
        up_parts.append(jnp.dot(rows.T, linear_grad, preferred_element_type=F32))
        down_parts.append(jnp.dot(active.T, scaled, preferred_element_type=F32))

    layer_output, token_grad = scatter_rows(out_rows, grad_rows, spread, rows_of)

    by_slot = jnp.concatenate(
        [
            gate_rows[0].reshape(2, SIDE, SIDE, HOT),
            gate_rows[1].reshape(2, SIDE, SIDE, COLD),
            gate_rows[2].reshape(2, SIDE, COPY_U)[:, :, : SIDE * COPY].reshape(2, SIDE, SIDE, COPY),
        ],
        axis=-1,
    )
    by_source = jnp.stack([by_slot[0], jnp.swapaxes(by_slot[1], 0, 1)], axis=2)
    by_source = jnp.pad(
        by_source.reshape(devices, HOT + COLD + COPY), ((0, 0), (0, 128 - HOT - COLD - COPY))
    )
    back = lax.all_to_all(by_source, "expert", split_axis=0, concat_axis=0, tiled=True)
    gate_grad = gate_back(dest, slot, back)

    own_first = hot_slot == 0

    def own(parts):
        return jnp.stack(
            [jnp.where(own_first, parts[0], parts[1]), jnp.where(own_first, parts[1], parts[0])]
        ).astype(BF)

    up_sum = lax.psum_scatter(own(up_parts), "dp", scatter_dimension=1, tiled=True)
    down_sum = lax.psum_scatter(own(down_parts), "dp", scatter_dimension=2, tiled=True)
    copy_up_sum = lax.psum_scatter(up_parts[2].astype(BF), "dp", scatter_dimension=0, tiled=True)
    copy_down_sum = lax.psum_scatter(
        down_parts[2].astype(BF), "dp", scatter_dimension=1, tiled=True
    )
    path = [((i + 1) % devices, i) for i in range(devices)]
    extra_up = lax.ppermute(copy_up_sum, "expert", path).astype(F32)
    extra_down = lax.ppermute(copy_down_sum, "expert", path).astype(F32)
    chosen = (jnp.arange(2, dtype=jnp.int32) == hot_slot).astype(F32)[:, None, None]
    up_grad = (up_sum.astype(F32) + chosen * extra_up[None]).astype(BF)
    down_grad = (down_sum.astype(F32) + chosen * extra_down[None]).astype(BF)
    return layer_output, token_grad, gate_grad, up_grad, down_grad


def solution(mesh):
    rows = P(("expert", "dp"), None)
    held = P("expert", None, None)
    return jax.shard_map(
        local,
        mesh=mesh,
        in_specs=(rows,) * 5 + (P(),) + (held,) * 4,
        out_specs=(rows, rows, rows, P("expert", "dp", None), P("expert", None, "dp")),
        check_vma=False,
    )
```

```python
import functools

import jax
import jax.numpy as jnp
from jax import lax
from jax.experimental import pallas as pl
from jax.experimental.pallas import tpu as pltpu
from jax.sharding import PartitionSpec as P

SIDE = 4
HOT, COLD, COPY = 24, 12, 6
SLOTS = 48
REPLICAS = 8
DEVICES = 2 * SIDE * SIDE
HOT_U, COLD_U, COPY_U = SIDE * HOT, SIDE * COLD, 32
UNIT = HOT_U + COLD_U + COPY_U
SPANS = ((0, HOT_U), (HOT_U, COLD_U), (HOT_U + COLD_U, COPY_U))
BF = jnp.bfloat16
F32 = jnp.float32
EXACT = lax.Precision.HIGHEST


def iota(shape, dim):
    return lax.broadcasted_iota(jnp.int32, shape, dim)


def route_kernel(ids_ref, picks_ref, gates_ref, listed_ref, table_ref, dest_ref, slot_ref):
    chosen, rows = ids_ref.shape
    ids, picks, gates = ids_ref[...], picks_ref[...], gates_ref[...]
    listed = listed_ref[...]
    devices = listed.shape[0]
    before = (iota((rows, rows), 0) < iota((rows, rows), 1)).astype(BF)
    lines = iota((128, rows), 0)
    token = iota((128, rows), 1).astype(F32) + 1.0
    offset = jnp.zeros((128, 1), F32)
    table = jnp.zeros((devices, 128), F32)
    for k in range(chosen):
        e, p, g = ids[k : k + 1], picks[k : k + 1], gates[k : k + 1]
        hot = jnp.max((e == listed).astype(jnp.int32), axis=0, keepdims=True)
        dest = (e // 2 + p) % devices
        region = jnp.where(p == 1, 2, 1 - hot)
        hit = (region * devices + dest == lines).astype(F32)
        ahead = jnp.dot(hit.astype(BF), before, preferred_element_type=F32) + offset
        rank = jnp.sum(hit * ahead, axis=0, keepdims=True).astype(jnp.int32)
        offset = offset + jnp.sum(hit, axis=1, keepdims=True)
        base = jnp.where(region == 0, 0, jnp.where(region == 1, HOT, HOT + COLD))
        slot = base + rank
        to = (dest == iota((devices, rows), 0)).astype(F32)
        value = jnp.where(slot == lines, token, 0.0) + jnp.where(slot + 64 == lines, g, 0.0)
        table = table + across(to, value, EXACT)
        dest_ref[k : k + 1] = dest
        slot_ref[k : k + 1] = slot
    table_ref[...] = table


def across(a, b, precision=None):
    return lax.dot_general(
        a, b, (((1,), (1,)), ((), ())), precision=precision, preferred_element_type=F32
    )


def route(ids, picks, gates, listed):
    chosen, rows = ids.shape
    vmem = pl.BlockSpec(memory_space=pltpu.VMEM)
    return pl.pallas_call(
        route_kernel,
        out_shape=(
            jax.ShapeDtypeStruct((listed.shape[0], 128), F32),
            jax.ShapeDtypeStruct((chosen, rows), jnp.int32),
            jax.ShapeDtypeStruct((chosen, rows), jnp.int32),
        ),
        in_specs=[vmem] * 4,
        out_specs=(vmem,) * 3,
        name="route",
    )(ids, picks, gates, listed.reshape(-1, 1))


def gate_kernel(dest_ref, slot_ref, back_ref, out_ref):
    chosen, rows = dest_ref.shape
    devices = back_ref.shape[0]
    back = jnp.transpose(back_ref[...])
    for k in range(chosen):
        to = (dest_ref[k : k + 1] == iota((devices, rows), 0)).astype(F32)
        picked = jnp.dot(back, to, precision=EXACT, preferred_element_type=F32)
        mine = jnp.where(slot_ref[k : k + 1] == iota((128, rows), 0), picked, 0.0)
        out_ref[k : k + 1] = jnp.sum(mine, axis=0, keepdims=True)


def gate_back(dest, slot, back):
    vmem = pl.BlockSpec(memory_space=pltpu.VMEM)
    return pl.pallas_call(
        gate_kernel,
        out_shape=jax.ShapeDtypeStruct(dest.shape, F32),
        in_specs=[vmem] * 3,
        out_specs=vmem,
        name="gate_back",
    )(dest, slot, back)


def serve_kernel(
    which_ref, hot_t, cold_t, copy_t, hot_c, cold_c, copy_c, gates_ref, up_ref, down_ref,
    copy_up_ref, copy_down_ref, hot_o, cold_o, copy_o, hot_g, cold_g, copy_g, grads_ref, back_ref,
    x, c, u, v, o, q, w, linear, slope, active, sums, in_sem, out_sem,
):
    firsts = (0, hot_t.shape[0], hot_t.shape[0] + cold_t.shape[0])
    counts = (hot_t.shape[0], cold_t.shape[0], copy_t.shape[0])
    width = x.shape[1]
    step = 512
    hot = which_ref[0]
    ups = (up_ref.at[hot], up_ref.at[1 - hot], copy_up_ref.at[0])
    downs = (down_ref.at[hot], down_ref.at[1 - hot], copy_down_ref.at[0])

    def loads(r):
        span = pl.ds(firsts[r], counts[r])
        pairs = (
            ((hot_t, cold_t, copy_t)[r], x.at[span]),
            (ups[r], u.at[r]),
            (downs[r], v.at[r]),
            ((hot_c, cold_c, copy_c)[r], c.at[span]),
        )
        return [pltpu.make_async_copy(*pair, in_sem.at[r, i]) for i, pair in enumerate(pairs)]

    stores = []

    def store(src, dst, r, i):
        copy = pltpu.make_async_copy(src, dst, out_sem.at[r, i])
        copy.start()
        stores.append(copy)

    for r in (2, 1, 0):
        for copy in loads(r):
            copy.start()
    for r in (2, 1, 0):
        first, count = firsts[r], counts[r]
        span = pl.ds(first, count)
        ready = loads(r)
        gate = jnp.transpose(jnp.broadcast_to(gates_ref[:, first : first + count], (128, count)))
        gate = gate[:, :1]
        ready[0].wait()
        ready[1].wait()
        tile = min(count, 384)

        @pl.loop(0, count // tile)
        def _(i):
            rows = pl.ds(pl.multiple_of(i * tile, tile), tile)
            value = jnp.dot(
                x[pl.ds(pl.multiple_of(first + i * tile, 128), tile)], u[r],
                preferred_element_type=F32)
            sigma = 1.0 / (1.0 + jnp.exp(-value))
            slope[rows] = sigma * (1.0 + value * (1.0 - sigma))
            active[rows] = (value * sigma).astype(BF)
            linear[rows] = value * sigma

        sums[pl.ds(0, count)] = jnp.zeros((count, 128), F32)
        ready[2].wait()
        ready[3].wait()

        @pl.loop(0, width // step)
        def _(j):
            cols = pl.ds(pl.multiple_of(j * step, step), step)
            served = jnp.dot(
                active[pl.ds(0, count)], v[r, :, cols], preferred_element_type=F32
            )
            cot = c[span, cols].astype(F32)
            both = served * cot
            part = both[:, :128]
            for i in range(1, step // 128):
                part = part + both[:, i * 128 : (i + 1) * 128]
            sums[pl.ds(0, count)] += part
            o[span, cols] = (gate * served).astype(BF)
            c[span, cols] = (gate * cot).astype(BF)

        store(o.at[span], (hot_o, cold_o, copy_o)[r], r, 0)

        @pl.loop(0, count // tile)
        def _(i):
            rows = pl.ds(pl.multiple_of(i * tile, tile), tile)
            value = across(c[pl.ds(pl.multiple_of(first + i * tile, 128), tile)], v[r])
            slope[rows] = value * slope[rows]

        flat = jnp.sum(sums[pl.ds(0, count)], axis=1, keepdims=True)
        flat = jnp.transpose(jnp.broadcast_to(flat, (count, 128)))
        back_ref[:, first : first + count] = flat[:1]
        slanted = slope[pl.ds(0, count)]
        linear_grad = slanted.astype(BF)
        turned = jnp.transpose(slanted).astype(BF)
        active_turned = jnp.transpose(linear[pl.ds(0, count)]).astype(BF)

        @pl.loop(0, width // step)
        def _(j):
            cols = pl.ds(pl.multiple_of(j * step, step), step)
            q[span, cols] = across(linear_grad, u[r, cols]).astype(BF)
            w[r, :, cols] = jnp.dot(turned, x[span, cols], preferred_element_type=F32).astype(BF)
            w[3 + r, :, cols] = jnp.dot(
                active_turned, c[span, cols], preferred_element_type=F32
            ).astype(BF)

        store(q.at[span], (hot_g, cold_g, copy_g)[r], r, 1)
        store(w.at[r], grads_ref.at[r], r, 2)
        store(w.at[3 + r], grads_ref.at[3 + r], r, 3)
    for copy in stores:
        copy.wait()


def serve(hot, gathered, gates, up_weight, down_weight, copy_up, copy_down):
    width, hidden = up_weight.shape[1:]
    counts = [rows.shape[0] for rows in gathered[:3]]
    total = sum(counts)
    anywhere = pl.BlockSpec(memory_space=pl.ANY)
    vmem = pl.BlockSpec(memory_space=pltpu.VMEM)
    rows = [jax.ShapeDtypeStruct((count, width), BF) for count in counts]
    return pl.pallas_call(
        serve_kernel,
        out_shape=(
            *rows, *rows, jax.ShapeDtypeStruct((6, hidden, width), BF),
            jax.ShapeDtypeStruct((1, total), F32),
        ),
        in_specs=[pl.BlockSpec(memory_space=pltpu.SMEM)] + [anywhere] * 6 + [vmem] + [anywhere] * 4,
        out_specs=(anywhere,) * 7 + (vmem,),
        scratch_shapes=[
            pltpu.VMEM((total, width), BF),
            pltpu.VMEM((total, width), BF),
            pltpu.VMEM((3, width, hidden), BF),
            pltpu.VMEM((3, hidden, width), BF),
            pltpu.VMEM((total, width), BF),
            pltpu.VMEM((total, width), BF),
            pltpu.VMEM((6, hidden, width), BF),
            pltpu.VMEM((counts[0], hidden), F32),
            pltpu.VMEM((counts[0], hidden), F32),
            pltpu.VMEM((counts[0], hidden), BF),
            pltpu.VMEM((counts[0], 128), F32),
            pltpu.SemaphoreType.DMA((3, 4)),
            pltpu.SemaphoreType.DMA((3, 4)),
        ],
        compiler_params=pltpu.CompilerParams(vmem_limit_bytes=62 << 20),
        name="serve",
    )(hot, *gathered, gates, up_weight, down_weight, copy_up, copy_down)


class Place:
    def __init__(self):
        me = lax.axis_index("expert")
        self.me = me
        self.core = me % 2
        x = (me // 2) % SIDE
        y = me // (2 * SIDE)
        self.s = x * (1 - self.core) + y * self.core
        self.b = y * (1 - self.core) + x * self.core

    def at(self, db, ds):
        b = (self.b + db + SIDE) % SIDE
        s = (self.s + ds + SIDE) % SIDE
        y = b * (1 - self.core) + s * self.core
        x = s * (1 - self.core) + b * self.core
        return {"expert": (y * SIDE + x) * 2 + self.core}

    def partner(self):
        return {"expert": self.me + 1 - 2 * self.core}

    def replica(self, dz):
        return {"dp": (lax.axis_index("dp") + dz + REPLICAS) % REPLICAS}

    def before(self):
        return {"expert": (self.me + DEVICES - 1) % DEVICES}

    def beyond(self):
        return {"expert": (self.me + DEVICES - 1 + 2 * self.core) % DEVICES}


def greet(place, *more):
    barrier = pltpu.get_barrier_semaphore()
    others = [place.at(0, 1), place.at(0, -1), place.at(1, 0), place.at(-1, 0), place.partner()]
    others.extend(more)
    for other in others:
        pl.semaphore_signal(barrier, inc=1, device_id=other, device_id_type=pl.DeviceIdType.MESH)
    pl.semaphore_wait(barrier, len(others))


def remote(src, dst, send, recv, device):
    return pltpu.make_async_remote_copy(
        src_ref=src,
        dst_ref=dst,
        send_sem=send,
        recv_sem=recv,
        device_id=device,
        device_id_type=pl.DeviceIdType.MESH,
    )


def gather_kernel(
    tok_ref, cot_ref, pick_ref, hot_t, cold_t, copy_t, hot_c, cold_c, copy_c,
    held, rows, own_sem, send, recv, out_sem,
):
    place = Place()
    rows_of = tok_ref.shape[0]
    half = rows_of // 2
    width = tok_ref.shape[1]
    sources = (tok_ref, cot_ref)
    outs = ((hot_t, cold_t, copy_t), (hot_c, cold_c, copy_c))
    started = []
    greet(place)

    def start(copy):
        copy.start()
        started.append(copy)
        return copy

    def spot(a, db, ds, part=None):
        b = (place.b + db + SIDE) % SIDE
        s = (place.s + ds + SIDE) % SIDE
        first = pl.multiple_of(s * rows_of, rows_of)
        if part is None:
            return held.at[a, b, pl.ds(first, rows_of)]
        return held.at[a, b, pl.ds(pl.multiple_of(first + part * half, half), half)]

    def full_s(a, sign):
        return remote(
            sources[a], spot(a, 0, 0), send.at[0, 0, (1 - sign) // 2, a, 0],
            recv.at[0, 0, (1 - sign) // 2, a, 0], place.at(0, sign))

    def half_s(a, sign):
        part = (1 - sign) // 2
        return remote(
            spot(a, 0, -sign, part), spot(a, 0, -sign, part), send.at[1, 0, part, a, 0],
            recv.at[1, 0, part, a, 0], place.at(0, sign))

    def full_b(a, sign, ds):
        src = sources[a] if ds == 0 else spot(a, 0, ds)
        return remote(
            src, spot(a, 0, ds), send.at[0, 1, (1 - sign) // 2, a, ds % SIDE],
            recv.at[0, 1, (1 - sign) // 2, a, ds % SIDE], place.at(sign, 0))

    def half_b(a, sign, ds):
        part = (1 - sign) // 2
        return remote(
            spot(a, -sign, ds, part), spot(a, -sign, ds, part),
            send.at[1, 1, part, a, ds % SIDE], recv.at[1, 1, part, a, ds % SIDE],
            place.at(sign, 0))

    def pick(db):
        b = (place.b + db + SIDE) % SIDE
        slot = db % SIDE
        to = place.core * SIDE + b
        for a in range(2):

            @pl.loop(0, width // 512)
            def _(j):
                cols = pl.ds(pl.multiple_of(j * 512, 512), 512)
                rows[slot, a, :, cols] = jnp.dot(
                    pick_ref[b], held[a, b, :, cols], preferred_element_type=F32
                ).astype(BF)

            for r, (first, count) in enumerate(SPANS):
                copy = pltpu.make_async_copy(
                    rows.at[slot, a, pl.ds(first, count)], outs[a][r].at[to],
                    out_sem.at[0, slot, a, r])
                copy.start()
                kept.append(copy)
                start(
                    remote(
                        rows.at[slot, a, pl.ds(UNIT + first, count)], outs[a][r].at[to],
                        out_sem.at[1, slot, a, r], out_sem.at[2, slot, a, r],
                        place.partner()))

    kept = []
    for a in range(2):
        for sign in (1, -1):
            start(full_s(a, sign))
        for sign in (1, -1):
            start(full_b(a, sign, 0))
    for a in range(2):
        copy = pltpu.make_async_copy(sources[a], spot(a, 0, 0), own_sem.at[a])
        copy.start()
        kept.append(copy)
    for a in range(2):
        for sign in (1, -1):
            full_s(a, sign).wait_recv()
            start(half_s(a, sign))
            for way in (1, -1):
                start(full_b(a, way, -sign))
        for sign in (1, -1):
            full_b(a, sign, 0).wait_recv()
            start(half_b(a, sign, 0))
    for a in range(2):
        for sign in (1, -1):
            half_s(a, sign).wait_recv()
        for way in (1, -1):
            start(full_b(a, way, 2))
    for copy in kept:
        copy.wait()
    kept = []
    pick(0)
    for a in range(2):
        for ds in (-1, 1):
            for sign in (1, -1):
                full_b(a, sign, ds).wait_recv()
                start(half_b(a, sign, ds))
    for a in range(2):
        for sign in (1, -1):
            full_b(a, sign, 2).wait_recv()
            start(half_b(a, sign, 2))
    pick(1)
    pick(-1)
    for a in range(2):
        for ds in (0, -1, 1, 2):
            for sign in (1, -1):
                half_b(a, sign, ds).wait_recv()
    pick(2)
    for copy in kept:
        copy.wait()
    for slot in range(SIDE):
        for a in range(2):
            b = (place.b + slot) % SIDE
            to = (1 - place.core) * SIDE + b
            for r, (first, count) in enumerate(SPANS):
                remote(
                    rows.at[slot, a, pl.ds(UNIT + first, count)], outs[a][r].at[to],
                    out_sem.at[1, slot, a, r], out_sem.at[2, slot, a, r],
                    place.partner()).wait_recv()
    for copy in started:
        copy.wait_send()


def gather_rows(tokens, cotangent, picks):
    width = tokens.shape[1]
    rows_of = tokens.shape[0]
    shapes = [jax.ShapeDtypeStruct((2 * SIDE, count, width), BF) for _, count in SPANS]
    anywhere = pl.BlockSpec(memory_space=pl.ANY)
    return pl.pallas_call(
        gather_kernel,
        out_shape=tuple(shapes + shapes),
        in_specs=[anywhere, anywhere, pl.BlockSpec(memory_space=pltpu.VMEM)],
        out_specs=(anywhere,) * 6,
        scratch_shapes=[
            pltpu.VMEM((2, SIDE, SIDE * rows_of, width), BF),
            pltpu.VMEM((SIDE, 2, 2 * UNIT, width), BF),
            pltpu.SemaphoreType.DMA((2,)),
            pltpu.SemaphoreType.DMA((2, 2, 2, 2, SIDE)),
            pltpu.SemaphoreType.DMA((2, 2, 2, 2, SIDE)),
            pltpu.SemaphoreType.DMA((3, SIDE, 2, 3)),
        ],
        compiler_params=pltpu.CompilerParams(
            collective_id=0, has_side_effects=True, vmem_limit_bytes=60 << 20
        ),
        name="gather_rows",
    )(tokens, cotangent, picks)


def scatter_kernel(
    hot_o, cold_o, copy_o, hot_g, cold_g, copy_g, spread_ref, grads_ref,
    out_ref, grad_ref, up_ref, down_ref,
    rows, sums, first_in, second_in, third_in, fourth_in, parts, ring_in, copy_in,
    in_sem, send_r, recv_r, send_1, recv_1, send_2, recv_2, send_3, recv_3, send_4, recv_4,
    part_sem, send_z, recv_z, send_c, recv_c,
):
    place = Place()
    width = out_ref.shape[1]
    rows_of = out_ref.shape[0]
    half = rows_of // 2
    ins = ((hot_o, cold_o, copy_o), (hot_g, cold_g, copy_g))
    order = (2, 3, 1, 0)
    started = []
    greet(place, place.replica(1), place.replica(-1), place.beyond())

    def start(copy):
        copy.start()
        started.append(copy)

    def part_copy(d):
        z = (lax.axis_index("dp") + d) % REPLICAS
        piece = parts.shape[-1]
        return pltpu.make_async_copy(
            grads_ref.at[:, :, pl.ds(pl.multiple_of(z * piece, piece), piece)], parts.at[d],
            part_sem.at[d])

    def ring(sign, k, p):
        way = (1 - sign) // 2
        spot = p % 3 if k == 1 else 6 * k - 9 + p
        return remote(
            parts.at[(sign * (5 - k)) % REPLICAS, p], ring_in.at[way, spot],
            send_z.at[way, spot], recv_z.at[way, spot], place.replica(sign))

    def later(sign):
        return (0, 1, 2) if sign == 1 else (3, 4, 5)

    def ring_start():
        for d in (4, 3, 5, 2, 6, 1, 7, 0):
            part_copy(d).start()
        part_copy(4).wait()
        for i in range(3):
            for sign in (1, -1):
                start(ring(sign, 1, later(sign)[i]))
        part_copy(3).wait()
        part_copy(5).wait()
        for i in range(3):
            for sign in (1, -1):
                start(ring(sign, 2, later(-sign)[i]))
        for d in (2, 6, 1, 7, 0):
            part_copy(d).wait()

    def ring_step(k, second):
        for i in range(3):
            for sign in (1, -1):
                p = later(sign if second else -sign)[i]
                ring(sign, k, p).wait_recv()
                spot = p % 3 if k == 1 else 6 * k - 9 + p
                add(parts.at[(sign * (4 - k)) % REPLICAS, p], ring_in.at[(1 - sign) // 2, spot])
                start(ring(sign, k + 1, p))

    def hand_over(i):
        return remote(
            parts.at[0, 3 * i + 2], copy_in.at[i], send_c.at[i], recv_c.at[i], place.before())

    def ring_end(p):
        for sign in (1, -1):
            ring(sign, 4, p).wait_recv()
        spot = 15 + p
        if p % 3 == 2:
            add(parts.at[0, p], ring_in.at[0, spot], ring_in.at[1, spot])
            start(hand_over(p // 3))
            return
        total = parts[0, p].astype(F32)
        for way in range(2):
            total = total + ring_in[way, spot].astype(F32)
        if p % 3 == 0:
            hand_over(p // 3).wait_recv()
            total = total + copy_in[p // 3].astype(F32)
        if p < 3:
            up_ref[p] = jnp.transpose(total).astype(BF)
        else:
            down_ref[p - 3] = total.astype(BF)

    def unit_copies(slot, a, r):
        first, count = SPANS[r]
        b = (place.b + slot) % SIDE
        return pltpu.make_async_copy(
            ins[a][r].at[place.core * SIDE + b], rows.at[slot, a, pl.ds(first, count)],
            in_sem.at[slot, a, r])

    def unit_sends(slot, a, r):
        first, count = SPANS[r]
        b = (place.s + slot) % SIDE
        return remote(
            ins[a][r].at[(1 - place.core) * SIDE + b],
            rows.at[slot, a, pl.ds(UNIT + first, count)],
            send_r.at[slot, a, r], recv_r.at[slot, a, r], place.partner())

    def chunk(slot, a, ds, part=None):
        s = (place.s + ds + SIDE) % SIDE
        first = pl.multiple_of(s * rows_of, rows_of)
        if part is None:
            return sums.at[slot, a, pl.ds(first, rows_of)]
        return sums.at[slot, a, pl.ds(pl.multiple_of(first + part * half, half), half)]

    def far(slot, a, sign):
        part = (1 - sign) // 2
        return remote(
            chunk(slot, a, 2, part), first_in.at[slot, a, part],
            send_1.at[slot, a, part], recv_1.at[slot, a, part], place.at(0, sign))

    def near(slot, a, sign, part):
        way = (1 - sign) // 2
        return remote(
            chunk(slot, a, sign, part), second_in.at[slot, a, way, pl.ds(part * half, half)],
            send_2.at[slot, a, way, part], recv_2.at[slot, a, way, part],
            place.at(0, sign))

    def far_b(a, sign):
        part = (1 - sign) // 2
        return remote(
            chunk(2, a, 0, part), third_in.at[a, part],
            send_3.at[a, part], recv_3.at[a, part], place.at(sign, 0))

    def near_b(a, sign, part):
        way = (1 - sign) // 2
        return remote(
            chunk(sign % SIDE, a, 0, part), fourth_in.at[a, way, pl.ds(part * half, half)],
            send_4.at[a, way, part], recv_4.at[a, way, part], place.at(sign, 0))

    def add(into, *others):
        @pl.loop(0, into.shape[0] // 32)
        def _(i):
            span = pl.ds(pl.multiple_of(i * 32, 32), 32)
            total = into[span].astype(F32)
            for other in others:
                total = total + other[span].astype(F32)
            into[span] = total.astype(BF)

    for slot in order:
        for a in range(2):
            for r in range(3):
                start(unit_sends(slot, a, r))
                unit_copies(slot, a, r).start()

    def expand(slot):
        b = (place.b + slot) % SIDE
        for a in range(2):
            for r in range(3):
                unit_copies(slot, a, r).wait()
                unit_sends(slot, a, r).wait_recv()

            @pl.loop(0, width // 512)
            def _(j):
                cols = pl.ds(pl.multiple_of(j * 512, 512), 512)
                sums[slot, a, :, cols] = jnp.dot(
                    spread_ref[b], rows[slot, a, :, cols], preferred_element_type=F32
                ).astype(BF)

            for sign in (1, -1):
                start(far(slot, a, sign))
            for sign in (1, -1):
                start(near(slot, a, sign, (1 + sign) // 2))

    def pass_on(slot):
        for a in range(2):
            for sign in (1, -1):
                part = (1 - sign) // 2
                far(slot, a, sign).wait_recv()
                add(chunk(slot, a, sign, part), first_in.at[slot, a, part])
                start(near(slot, a, sign, part))

    def finish(slot):
        for a in range(2):
            for sign in (1, -1):
                for part in range(2):
                    near(slot, a, sign, part).wait_recv()
            add(chunk(slot, a, 0), second_in.at[slot, a, 0], second_in.at[slot, a, 1])

    ring_start()
    expand(2)
    expand(3)
    pass_on(2)
    ring_step(1, True)
    expand(1)
    ring_step(2, False)
    pass_on(3)
    finish(2)
    for a in range(2):
        for sign in (1, -1):
            start(far_b(a, sign))
    expand(0)
    ring_step(2, True)
    pass_on(1)
    finish(3)
    for a in range(2):
        start(near_b(a, -1, 0))
    ring_step(3, False)
    pass_on(0)
    finish(1)
    for a in range(2):
        start(near_b(a, 1, 1))
    ring_step(3, True)
    for a in range(2):
        for sign in (1, -1):
            part = (1 - sign) // 2
            far_b(a, sign).wait_recv()
            add(chunk(sign % SIDE, a, 0, part), third_in.at[a, part])
            start(near_b(a, sign, part))
    finish(0)
    for p in (5, 2):
        ring_end(p)
    for a, result in ((0, out_ref), (1, grad_ref)):
        for sign in (1, -1):
            for part in range(2):
                near_b(a, sign, part).wait_recv()
        own = chunk(0, a, 0)
        result[...] = (
            own[...].astype(F32) + fourth_in[a, 0].astype(F32) + fourth_in[a, 1].astype(F32)
        ).astype(BF)
    for p in (4, 1, 3, 0):
        ring_end(p)
    for copy in started:
        copy.wait_send()


def scatter_rows(out_rows, grad_rows, spread, grads, rows_of):
    width = out_rows[0].shape[-1]
    hidden = grads.shape[1]
    piece = width // REPLICAS
    half = rows_of // 2
    anywhere = pl.BlockSpec(memory_space=pl.ANY)
    vmem = pl.BlockSpec(memory_space=pltpu.VMEM)
    shape = jax.ShapeDtypeStruct((rows_of, width), BF)
    dma = pltpu.SemaphoreType.DMA
    return pl.pallas_call(
        scatter_kernel,
        out_shape=(
            shape, shape, jax.ShapeDtypeStruct((2, piece, hidden), BF),
            jax.ShapeDtypeStruct((2, hidden, piece), BF),
        ),
        in_specs=[anywhere] * 6 + [vmem, anywhere],
        out_specs=(vmem,) * 4,
        scratch_shapes=[
            pltpu.VMEM((SIDE, 2, 2 * UNIT, width), BF),
            pltpu.VMEM((SIDE, 2, SIDE * rows_of, width), BF),
            pltpu.VMEM((SIDE, 2, 2, half, width), BF),
            pltpu.VMEM((SIDE, 2, 2, rows_of, width), BF),
            pltpu.VMEM((2, 2, half, width), BF),
            pltpu.VMEM((2, 2, rows_of, width), BF),
            pltpu.VMEM((REPLICAS, 6, hidden, piece), BF),
            pltpu.VMEM((2, 21, hidden, piece), BF),
            pltpu.VMEM((2, hidden, piece), BF),
            dma((SIDE, 2, 3)),
            dma((SIDE, 2, 3)),
            dma((SIDE, 2, 3)),
            dma((SIDE, 2, 2)),
            dma((SIDE, 2, 2)),
            dma((SIDE, 2, 2, 2)),
            dma((SIDE, 2, 2, 2)),
            dma((2, 2)),
            dma((2, 2)),
            dma((2, 2, 2)),
            dma((2, 2, 2)),
            dma((REPLICAS,)),
            dma((2, 21)),
            dma((2, 21)),
            dma((2,)),
            dma((2,)),
        ],
        compiler_params=pltpu.CompilerParams(
            collective_id=1, has_side_effects=True, vmem_limit_bytes=67043328
        ),
        name="scatter_rows",
    )(*out_rows, *grad_rows, spread, grads)


def regions(values, fill):
    lead = values.shape[:-2]
    hot = values[..., :HOT].reshape(*lead, HOT_U)
    cold = values[..., HOT : HOT + COLD].reshape(*lead, COLD_U)
    copied = values[..., HOT + COLD : HOT + COLD + COPY].reshape(*lead, SIDE * COPY)
    pad = [(0, 0)] * len(lead) + [(0, COPY_U - SIDE * COPY)]
    return hot, cold, jnp.pad(copied, pad, constant_values=fill)


def local(
    tokens,
    cotangent,
    gate_weights,
    expert_ids,
    copy_pick,
    copy_expert,
    up_weight,
    down_weight,
    copy_up,
    copy_down,
):
    devices = lax.axis_size("expert")
    me = lax.axis_index("expert")
    core = me % 2
    rows_of, width = tokens.shape
    table, dest, slot = route(expert_ids.T, copy_pick.T, gate_weights.T, copy_expert)
    sent = jnp.broadcast_to(
        table.reshape(devices // 2, 1, 2, 128), (devices // 2, 2, 2, 128)
    ).reshape(devices, 2, 128)
    tables = lax.all_to_all(sent, "expert", split_axis=0, concat_axis=0, tiled=True)
    grid = tables.reshape(SIDE, SIDE, 2, 2, 128)
    by_unit = jnp.stack([grid[:, :, 0], jnp.swapaxes(grid[:, :, 1], 0, 1)])
    mine = jnp.where(core == 0, by_unit[:, :, :, 0], by_unit[:, :, :, 1])
    gates = regions(mine[..., 64 : 64 + SLOTS], 0.0)
    named = jnp.where(core == 0, by_unit[0], by_unit[1])[..., :SLOTS].astype(jnp.int32)
    named = jnp.where(core == 0, named, named[:, :, ::-1])
    place = jnp.arange(SIDE, dtype=jnp.int32)[None, :, None, None] * rows_of
    named = jnp.where(named > 0, place + named - 1, -1)
    named = jnp.concatenate(regions(jnp.moveaxis(named, 2, 1), -1), axis=-1)
    named = named.reshape(SIDE, 2 * UNIT)
    sites = jnp.arange(SIDE * rows_of, dtype=jnp.int32)
    picks = (named[:, :, None] == sites[None, None, :]).astype(BF)
    spread = (named[:, None, :] == sites[None, :, None]).astype(BF)

    gathered = gather_rows(tokens, cotangent, picks)
    hot_slot = copy_expert[(me + 1) % devices] % 2
    gates = jnp.concatenate([gate.reshape(1, -1) for gate in gates], axis=1)
    *rows, grads, back = serve(
        hot_slot.reshape(1),
        [part.reshape(-1, width) for part in gathered],
        gates, up_weight, down_weight, copy_up, copy_down,
    )
    rows = [part.reshape(2 * SIDE, -1, width) for part in rows]
    layer_output, token_grad, up_parts, down_parts = scatter_rows(
        rows[:3], rows[3:], spread, grads, rows_of
    )

    hot_back, cold_back, copy_back = jnp.split(
        back[0], [2 * SIDE * HOT_U, 2 * SIDE * (HOT_U + COLD_U)]
    )
    by_slot = jnp.concatenate(
        [
            hot_back.reshape(2, SIDE, SIDE, HOT),
            cold_back.reshape(2, SIDE, SIDE, COLD),
            copy_back.reshape(2, SIDE, COPY_U)[:, :, : SIDE * COPY].reshape(2, SIDE, SIDE, COPY),
        ],
        axis=-1,
    )
    by_source = jnp.stack([by_slot[0], jnp.swapaxes(by_slot[1], 0, 1)], axis=2)
    by_source = jnp.pad(
        by_source.reshape(devices, HOT + COLD + COPY), ((0, 0), (0, 128 - HOT - COLD - COPY))
    )
    returned = lax.all_to_all(by_source, "expert", split_axis=0, concat_axis=0, tiled=True)
    gate_grad = gate_back(dest, slot, returned).T

    up_grad = jnp.where(hot_slot == 0, up_parts, up_parts[::-1])
    down_grad = jnp.where(hot_slot == 0, down_parts, down_parts[::-1])
    return layer_output, token_grad, gate_grad, up_grad, down_grad


def solution(mesh):
    rows = P(("expert", "dp"), None)
    held = P("expert", None, None)
    return jax.shard_map(
        local,
        mesh=mesh,
        in_specs=(rows,) * 5 + (P(),) + (held,) * 4,
        out_specs=(rows, rows, rows, P("expert", "dp", None), P("expert", None, "dp")),
        check_vma=False,
    )
```

```python
import functools

import jax
import jax.numpy as jnp
from jax import lax
from jax.experimental import pallas as pl
from jax.experimental.pallas import tpu as pltpu
from jax.sharding import PartitionSpec as P

SIDE = 4
HOT, COLD, COPY = 24, 12, 6
SLOTS = 48
REPLICAS = 8
DEVICES = 2 * SIDE * SIDE
HOT_U, COLD_U, COPY_U = SIDE * HOT, SIDE * COLD, 32
UNIT = HOT_U + COLD_U + COPY_U
SPANS = ((0, HOT_U), (HOT_U, COLD_U), (HOT_U + COLD_U, COPY_U))
BF = jnp.bfloat16
F32 = jnp.float32
EXACT = lax.Precision.HIGHEST


def iota(shape, dim):
    return lax.broadcasted_iota(jnp.int32, shape, dim)


def route_kernel(ids_ref, picks_ref, gates_ref, listed_ref, table_ref, dest_ref, slot_ref):
    chosen, rows = ids_ref.shape
    ids, picks, gates = ids_ref[...], picks_ref[...], gates_ref[...]
    devices = listed_ref.shape[0]
    cold = jnp.ones((chosen, rows), jnp.int32)
    for i in range(devices):
        cold = jnp.where(ids == listed_ref[i], 0, cold)
    before = (iota((rows, rows), 0) < iota((rows, rows), 1)).astype(BF)
    lines = iota((128, rows), 0)
    token = iota((128, rows), 1).astype(F32) + 1.0
    offset = jnp.zeros((128, 1), F32)
    table = jnp.zeros((devices, 128), F32)
    for k in range(chosen):
        e, p, g = ids[k : k + 1], picks[k : k + 1], gates[k : k + 1]
        dest = (e // 2 + p) % devices
        region = jnp.where(p == 1, 2, cold[k : k + 1])
        hit = (region * devices + dest == lines).astype(F32)
        ahead = jnp.dot(hit.astype(BF), before, preferred_element_type=F32) + offset
        rank = jnp.sum(hit * ahead, axis=0, keepdims=True).astype(jnp.int32)
        offset = offset + jnp.sum(hit, axis=1, keepdims=True)
        base = jnp.where(region == 0, 0, jnp.where(region == 1, HOT, HOT + COLD))
        slot = base + rank
        to = (dest == iota((devices, rows), 0)).astype(F32)
        value = jnp.where(slot == lines, token, 0.0) + jnp.where(slot + 64 == lines, g, 0.0)
        table = table + across(to, value, EXACT)
        dest_ref[k : k + 1] = dest
        slot_ref[k : k + 1] = slot
    table_ref[...] = table


def across(a, b, precision=None):
    return lax.dot_general(
        a, b, (((1,), (1,)), ((), ())), precision=precision, preferred_element_type=F32
    )


def route(ids, picks, gates, listed):
    chosen, rows = ids.shape
    vmem = pl.BlockSpec(memory_space=pltpu.VMEM)
    return pl.pallas_call(
        route_kernel,
        out_shape=(
            jax.ShapeDtypeStruct((listed.shape[0], 128), F32),
            jax.ShapeDtypeStruct((chosen, rows), jnp.int32),
            jax.ShapeDtypeStruct((chosen, rows), jnp.int32),
        ),
        in_specs=[vmem] * 3 + [pl.BlockSpec(memory_space=pltpu.SMEM)],
        out_specs=(vmem,) * 3,
        name="route",
    )(ids, picks, gates, listed)


def seats(s, rows, lead):
    row, lane = iota((rows, 128), 0), iota((rows, 128), 1) - lead
    hot = (row - HOT * s == lane) & (lane >= 0) & (lane < HOT)
    cold = (row - HOT_U - COLD * s == lane - HOT) & (lane >= HOT) & (lane < HOT + COLD)
    copied = (row - HOT_U - COLD_U - COPY * s == lane - HOT - COLD) & (lane >= HOT + COLD)
    copied = copied & (lane < HOT + COLD + COPY)
    return (hot | cold | copied).astype(F32)


def gate_kernel(dest_ref, slot_ref, back_ref, out_ref):
    chosen, rows = dest_ref.shape
    devices = back_ref.shape[0]
    back = jnp.transpose(back_ref[...])
    for k in range(chosen):
        to = (dest_ref[k : k + 1] == iota((devices, rows), 0)).astype(F32)
        picked = jnp.dot(back, to, precision=EXACT, preferred_element_type=F32)
        mine = jnp.where(slot_ref[k : k + 1] == iota((128, rows), 0), picked, 0.0)
        out_ref[k : k + 1] = jnp.sum(mine, axis=0, keepdims=True)


def gate_back(dest, slot, back):
    vmem = pl.BlockSpec(memory_space=pltpu.VMEM)
    return pl.pallas_call(
        gate_kernel,
        out_shape=jax.ShapeDtypeStruct(dest.shape, F32),
        in_specs=[vmem] * 3,
        out_specs=vmem,
        name="gate_back",
    )(dest, slot, back)


def serve_kernel(
    which_ref, hot_t, cold_t, copy_t, hot_c, cold_c, copy_c, gates_ref, up_ref, down_ref,
    copy_up_ref, copy_down_ref, hot_o, cold_o, copy_o, hot_g, cold_g, copy_g, grads_ref, back_ref,
    x, c, u, v, o, q, w, linear, slope, active, sums, gate_cols, by_unit, in_sem, out_sem,
):
    firsts = (0, hot_t.shape[0], hot_t.shape[0] + cold_t.shape[0])
    counts = (hot_t.shape[0], cold_t.shape[0], copy_t.shape[0])
    width = x.shape[1]
    step = 512
    me = lax.axis_index("expert")
    hot = which_ref[(me + 1) % DEVICES] % 2
    ups = (up_ref.at[hot], up_ref.at[1 - hot], copy_up_ref.at[0])
    downs = (down_ref.at[hot], down_ref.at[1 - hot], copy_down_ref.at[0])

    def loads(r):
        span = pl.ds(firsts[r], counts[r])
        pairs = (
            ((hot_t, cold_t, copy_t)[r], x.at[span]),
            (ups[r], u.at[r]),
            (downs[r], v.at[r]),
            ((hot_c, cold_c, copy_c)[r], c.at[span]),
        )
        return [pltpu.make_async_copy(*pair, in_sem.at[r, i]) for i, pair in enumerate(pairs)]

    stores = []

    def store(src, dst, r, i):
        copy = pltpu.make_async_copy(src, dst, out_sem.at[r, i])
        copy.start()
        stores.append(copy)

    for r in (2, 1, 0):
        for copy in loads(r):
            copy.start()
    for i in range(2 * SIDE):
        columns = jnp.transpose(jnp.broadcast_to(gates_ref[i, :1], (128, gates_ref.shape[2])))
        for r, (low, rows) in enumerate(SPANS):
            gate_cols[pl.ds(firsts[r] + i * rows, rows)] = columns[low : low + rows]
    by_unit[...] = jnp.zeros_like(by_unit)
    for r in (2, 1, 0):
        first, count = firsts[r], counts[r]
        span = pl.ds(first, count)
        ready = loads(r)
        gate = gate_cols[span][:, :1]
        ready[0].wait()
        ready[1].wait()
        tile = min(count, 384)

        @pl.loop(0, count // tile)
        def _(i):
            rows = pl.ds(pl.multiple_of(i * tile, tile), tile)
            value = jnp.dot(
                x[pl.ds(pl.multiple_of(first + i * tile, 128), tile)], u[r],
                preferred_element_type=F32)
            sigma = 1.0 / (1.0 + jnp.exp(-value))
            slope[rows] = sigma * (1.0 + value * (1.0 - sigma))
            active[rows] = (value * sigma).astype(BF)
            linear[rows] = value * sigma

        sums[pl.ds(0, count)] = jnp.zeros((count, 128), F32)
        ready[2].wait()
        ready[3].wait()

        @pl.loop(0, width // step)
        def _(j):
            cols = pl.ds(pl.multiple_of(j * step, step), step)
            served = jnp.dot(
                active[pl.ds(0, count)], v[r, :, cols], preferred_element_type=F32
            )
            cot = c[span, cols].astype(F32)
            both = served * cot
            part = both[:, :128]
            for i in range(1, step // 128):
                part = part + both[:, i * 128 : (i + 1) * 128]
            sums[pl.ds(0, count)] += part
            o[span, cols] = (gate * served).astype(BF)
            c[span, cols] = (gate * cot).astype(BF)

        store(o.at[span], (hot_o, cold_o, copy_o)[r], r, 0)

        @pl.loop(0, count // tile)
        def _(i):
            rows = pl.ds(pl.multiple_of(i * tile, tile), tile)
            value = across(c[pl.ds(pl.multiple_of(first + i * tile, 128), tile)], v[r])
            slope[rows] = value * slope[rows]

        low, rows = SPANS[r]
        totals = jnp.zeros((rows, 128), F32)
        for i in range(2 * SIDE):
            one = jnp.sum(sums[pl.ds(i * rows, rows)], axis=1, keepdims=True)
            totals = jnp.where(iota((rows, 128), 1) == i, one, totals)
        by_unit[pl.ds(low, rows)] = totals
        slanted = slope[pl.ds(0, count)]
        linear_grad = slanted.astype(BF)
        turned = jnp.transpose(slanted).astype(BF)
        active_turned = jnp.transpose(linear[pl.ds(0, count)]).astype(BF)

        @pl.loop(0, width // step)
        def _(j):
            cols = pl.ds(pl.multiple_of(j * step, step), step)
            q[span, cols] = across(linear_grad, u[r, cols]).astype(BF)
            w[r, :, cols] = jnp.dot(turned, x[span, cols], preferred_element_type=F32).astype(BF)
            w[3 + r, :, cols] = jnp.dot(
                active_turned, c[span, cols], preferred_element_type=F32
            ).astype(BF)

        store(q.at[span], (hot_g, cold_g, copy_g)[r], r, 1)
        store(w.at[r], grads_ref.at[r], r, 2)
        store(w.at[3 + r], grads_ref.at[3 + r], r, 3)
    turned = jnp.transpose(by_unit[...])
    for s in range(SIDE):
        lines = jnp.dot(
            turned, seats(s, by_unit.shape[0], 0), precision=EXACT, preferred_element_type=F32
        )
        for b in range(SIDE):
            for core in range(2):
                source = ((b * SIDE + s) if core == 0 else (s * SIDE + b)) * 2 + core
                i = core * SIDE + b
                back_ref[source : source + 1] = lines[i : i + 1]
    for copy in stores:
        copy.wait()


def serve(listed, gathered, gates, up_weight, down_weight, copy_up, copy_down):
    width, hidden = up_weight.shape[1:]
    counts = [rows.shape[0] for rows in gathered[:3]]
    total = sum(counts)
    anywhere = pl.BlockSpec(memory_space=pl.ANY)
    vmem = pl.BlockSpec(memory_space=pltpu.VMEM)
    rows = [jax.ShapeDtypeStruct((count, width), BF) for count in counts]
    return pl.pallas_call(
        serve_kernel,
        out_shape=(
            *rows, *rows, jax.ShapeDtypeStruct((6, hidden, width), BF),
            jax.ShapeDtypeStruct((DEVICES, 128), F32),
        ),
        in_specs=[pl.BlockSpec(memory_space=pltpu.SMEM)] + [anywhere] * 6 + [vmem] + [anywhere] * 4,
        out_specs=(anywhere,) * 7 + (vmem,),
        scratch_shapes=[
            pltpu.VMEM((total, width), BF),
            pltpu.VMEM((total, width), BF),
            pltpu.VMEM((3, width, hidden), BF),
            pltpu.VMEM((3, hidden, width), BF),
            pltpu.VMEM((total, width), BF),
            pltpu.VMEM((total, width), BF),
            pltpu.VMEM((6, hidden, width), BF),
            pltpu.VMEM((counts[0], hidden), F32),
            pltpu.VMEM((counts[0], hidden), F32),
            pltpu.VMEM((counts[0], hidden), BF),
            pltpu.VMEM((counts[0], 128), F32),
            pltpu.VMEM((total, 128), F32),
            pltpu.VMEM((256, 128), F32),
            pltpu.SemaphoreType.DMA((3, 4)),
            pltpu.SemaphoreType.DMA((3, 4)),
        ],
        compiler_params=pltpu.CompilerParams(vmem_limit_bytes=62 << 20),
        name="serve",
    )(listed, *gathered, gates, up_weight, down_weight, copy_up, copy_down)


class Place:
    def __init__(self):
        me = lax.axis_index("expert")
        self.me = me
        self.core = me % 2
        x = (me // 2) % SIDE
        y = me // (2 * SIDE)
        self.s = x * (1 - self.core) + y * self.core
        self.b = y * (1 - self.core) + x * self.core

    def at(self, db, ds):
        b = (self.b + db + SIDE) % SIDE
        s = (self.s + ds + SIDE) % SIDE
        y = b * (1 - self.core) + s * self.core
        x = s * (1 - self.core) + b * self.core
        return {"expert": (y * SIDE + x) * 2 + self.core}

    def partner(self):
        return {"expert": self.me + 1 - 2 * self.core}

    def replica(self, dz):
        return {"dp": (lax.axis_index("dp") + dz + REPLICAS) % REPLICAS}

    def before(self):
        return {"expert": (self.me + DEVICES - 1) % DEVICES}

    def beyond(self):
        return {"expert": (self.me + DEVICES - 1 + 2 * self.core) % DEVICES}


def greet(place, *more):
    barrier = pltpu.get_barrier_semaphore()
    others = [place.at(0, 1), place.at(0, -1), place.at(1, 0), place.at(-1, 0), place.partner()]
    others.extend(more)
    for other in others:
        pl.semaphore_signal(barrier, inc=1, device_id=other, device_id_type=pl.DeviceIdType.MESH)
    pl.semaphore_wait(barrier, len(others))


def remote(src, dst, send, recv, device):
    return pltpu.make_async_remote_copy(
        src_ref=src,
        dst_ref=dst,
        send_sem=send,
        recv_sem=recv,
        device_id=device,
        device_id_type=pl.DeviceIdType.MESH,
    )


def gather_kernel(
    tok_ref, cot_ref, table_ref, hot_t, cold_t, copy_t, hot_c, cold_c, copy_c, gates_ref, spread_ref,
    held, tables, rows, picks, spread, gates, own_sem, send, recv, out_sem, gate_sem, spread_sem,
):
    place = Place()
    rows_of = tok_ref.shape[0]
    width = tok_ref.shape[1]
    sources = (tok_ref, cot_ref, table_ref)
    outs = ((hot_t, cold_t, copy_t), (hot_c, cold_c, copy_c))
    started = []
    greet(place)

    def start(copy):
        copy.start()
        started.append(copy)
        return copy

    def spot(a, db, ds, part=None):
        b = (place.b + db + SIDE) % SIDE
        s = (place.s + ds + SIDE) % SIDE
        count = sources[a].shape[0]
        half = count // 2
        first = pl.multiple_of(s * count, count)
        within = tables.at[b] if a == 2 else held.at[a, b]
        if part is None:
            return within.at[pl.ds(first, count)]
        return within.at[pl.ds(pl.multiple_of(first + part * half, half), half)]

    def full_s(a, sign):
        return remote(
            sources[a], spot(a, 0, 0), send.at[0, 0, (1 - sign) // 2, a, 0],
            recv.at[0, 0, (1 - sign) // 2, a, 0], place.at(0, sign))

    def half_s(a, sign):
        part = (1 - sign) // 2
        return remote(
            spot(a, 0, -sign, part), spot(a, 0, -sign, part), send.at[1, 0, part, a, 0],
            recv.at[1, 0, part, a, 0], place.at(0, sign))

    def full_b(a, sign, ds):
        src = sources[a] if ds == 0 else spot(a, 0, ds)
        return remote(
            src, spot(a, 0, ds), send.at[0, 1, (1 - sign) // 2, a, ds % SIDE],
            recv.at[0, 1, (1 - sign) // 2, a, ds % SIDE], place.at(sign, 0))

    def half_b(a, sign, ds):
        part = (1 - sign) // 2
        return remote(
            spot(a, -sign, ds, part), spot(a, -sign, ds, part),
            send.at[1, 1, part, a, ds % SIDE], recv.at[1, 1, part, a, ds % SIDE],
            place.at(sign, 0))

    def plan(db):
        b = (place.b + db + SIDE) % SIDE
        slot = db % SIDE
        for h in range(2):
            target = place.me + h * (1 - 2 * place.core)
            scale = jnp.zeros((8, UNIT), F32)
            for s in range(SIDE):
                line = tables[b, pl.ds(s * DEVICES + target, 1), :]
                wide = jnp.broadcast_to(line, (128, 128))
                site = iota((128, 128), 1).astype(F32) + 1.0
                one = (jnp.transpose(wide) == site).astype(BF)
                turned = (wide == iota((128, 128), 0).astype(F32) + 1.0).astype(BF)
                seat = seats(s, UNIT, 0).astype(BF)
                span = pl.ds(s * rows_of, rows_of)
                picks[slot, h, :, span] = jnp.dot(seat, one, preferred_element_type=F32).astype(BF)
                spread[slot, h, span, :] = across(turned, seat).astype(BF)
                scale = scale + across(wide[:8], seats(s, UNIT, 64), EXACT)
            gates[slot, h, :, pl.ds(0, UNIT)] = scale
        unit = place.core * SIDE + b
        keep(pltpu.make_async_copy(gates.at[slot, 0], gates_ref.at[unit], gate_sem.at[0, slot]))
        start(gates_out(slot))
        keep(pltpu.make_async_copy(spread.at[slot], spread_ref.at[b], spread_sem.at[slot]))

    def gates_out(slot):
        b = (place.b + slot) % SIDE
        return remote(
            gates.at[slot, 1], gates_ref.at[place.core * SIDE + b], gate_sem.at[1, slot],
            gate_sem.at[2, slot], place.partner())

    def rows_out(slot, a, r):
        b = (place.b + slot) % SIDE
        first, count = SPANS[r]
        return remote(
            rows.at[slot, a, 1, pl.ds(first, count)], outs[a][r].at[place.core * SIDE + b],
            out_sem.at[1, slot, a, r], out_sem.at[2, slot, a, r], place.partner())

    def pick(db, a):
        b = (place.b + db + SIDE) % SIDE
        slot = db % SIDE
        for h in (1, 0):

            @pl.loop(0, width // 512)
            def _(j):
                cols = pl.ds(pl.multiple_of(j * 512, 512), 512)
                rows[slot, a, h, :, cols] = jnp.dot(
                    picks[slot, h], held[a, b, :, cols], preferred_element_type=F32
                ).astype(BF)

            for r, (first, count) in enumerate(SPANS):
                if h == 1:
                    start(rows_out(slot, a, r))
                else:
                    keep(
                        pltpu.make_async_copy(
                            rows.at[slot, a, 0, pl.ds(first, count)],
                            outs[a][r].at[place.core * SIDE + b], out_sem.at[0, slot, a, r]))

    kept = []

    def keep(copy):
        copy.start()
        kept.append(copy)

    arrays = (2, 0, 1)
    for a in arrays:
        for sign in (1, -1):
            start(full_s(a, sign))
        for sign in (1, -1):
            start(full_b(a, sign, 0))
    for a in arrays:
        keep(pltpu.make_async_copy(sources[a], spot(a, 0, 0), own_sem.at[a]))
    for a in arrays:
        for sign in (1, -1):
            full_s(a, sign).wait_recv()
            start(half_s(a, sign))
            for way in (1, -1):
                start(full_b(a, way, -sign))
        for sign in (1, -1):
            full_b(a, sign, 0).wait_recv()
            start(half_b(a, sign, 0))
    for a in arrays:
        for sign in (1, -1):
            half_s(a, sign).wait_recv()
        for way in (1, -1):
            start(full_b(a, way, 2))
    for copy in kept:
        copy.wait()
    kept.clear()
    plan(0)
    for a in range(2):
        pick(0, a)
    for ds in (-1, 1, 2):
        for a in arrays:
            for sign in (1, -1):
                full_b(a, sign, ds).wait_recv()
                start(half_b(a, sign, ds))
    for db in (1, -1):
        plan(db)
        for a in range(2):
            pick(db, a)
    for ds in (0, -1, 1, 2):
        for sign in (1, -1):
            half_b(2, sign, ds).wait_recv()
    plan(2)
    for a in range(2):
        for ds in (0, -1, 1, 2):
            for sign in (1, -1):
                half_b(a, sign, ds).wait_recv()
        pick(2, a)
    for copy in kept:
        copy.wait()
    for slot in range(SIDE):
        gates_out(slot).wait_recv()
        for a in range(2):
            for r in range(3):
                rows_out(slot, a, r).wait_recv()
    for copy in started:
        copy.wait_send()


def gather_rows(tokens, cotangent, table):
    width = tokens.shape[1]
    rows_of = tokens.shape[0]
    shapes = [jax.ShapeDtypeStruct((2 * SIDE, count, width), BF) for _, count in SPANS]
    dma = pltpu.SemaphoreType.DMA
    anywhere = pl.BlockSpec(memory_space=pl.ANY)
    return pl.pallas_call(
        gather_kernel,
        out_shape=(
            *shapes, *shapes, jax.ShapeDtypeStruct((2 * SIDE, 8, 256), F32),
            jax.ShapeDtypeStruct((SIDE, 2, SIDE * rows_of, UNIT), BF),
        ),
        in_specs=[anywhere] * 3,
        out_specs=(anywhere,) * 8,
        scratch_shapes=[
            pltpu.VMEM((2, SIDE, SIDE * rows_of, width), BF),
            pltpu.VMEM((SIDE, SIDE * DEVICES, 128), F32),
            pltpu.VMEM((SIDE, 2, 2, UNIT, width), BF),
            pltpu.VMEM((SIDE, 2, UNIT, SIDE * rows_of), BF),
            pltpu.VMEM((SIDE, 2, SIDE * rows_of, UNIT), BF),
            pltpu.VMEM((SIDE, 2, 8, 256), F32),
            dma((3,)),
            dma((2, 2, 2, 3, SIDE)),
            dma((2, 2, 2, 3, SIDE)),
            dma((3, SIDE, 2, 3)),
            dma((3, SIDE)),
            dma((SIDE,)),
        ],
        compiler_params=pltpu.CompilerParams(
            collective_id=0, has_side_effects=True, vmem_limit_bytes=60 << 20
        ),
        name="gather_rows",
    )(tokens, cotangent, table)


def scatter_kernel(
    hot_o, cold_o, copy_o, hot_g, cold_g, copy_g, spread_ref, grads_ref, first_ref,
    out_ref, grad_ref, up_ref, down_ref,
    rows, sums, first_in, second_in, third_in, fourth_in, parts, ring_in, copy_in, spread,
    in_sem, send_r, recv_r, send_1, recv_1, send_2, recv_2, send_3, recv_3, send_4, recv_4,
    part_sem, send_z, recv_z, send_c, recv_c, spread_sem,
):
    place = Place()
    width = out_ref.shape[1]
    rows_of = out_ref.shape[0]
    half = rows_of // 2
    ins = ((hot_o, cold_o, copy_o), (hot_g, cold_g, copy_g))
    order = (2, 3, 1, 0)
    started = []
    greet(place, place.replica(1), place.replica(-1), place.beyond())

    def start(copy):
        copy.start()
        started.append(copy)

    def part_copy(d):
        z = (lax.axis_index("dp") + d) % REPLICAS
        piece = parts.shape[-1]
        return pltpu.make_async_copy(
            grads_ref.at[:, :, pl.ds(pl.multiple_of(z * piece, piece), piece)], parts.at[d],
            part_sem.at[d])

    def ring(sign, k, p):
        way = (1 - sign) // 2
        spot = p % 3 if k == 1 else 6 * k - 9 + p
        return remote(
            parts.at[(sign * (5 - k)) % REPLICAS, p], ring_in.at[way, spot],
            send_z.at[way, spot], recv_z.at[way, spot], place.replica(sign))

    def later(sign):
        return (2, 0, 1) if sign == 1 else (5, 3, 4)

    def ring_start():
        for d in (4, 3, 5, 2, 6, 1, 7, 0):
            part_copy(d).start()
        part_copy(4).wait()
        for i in range(3):
            for sign in (1, -1):
                start(ring(sign, 1, later(sign)[i]))
        part_copy(3).wait()
        part_copy(5).wait()
        for i in range(3):
            for sign in (1, -1):
                start(ring(sign, 2, later(-sign)[i]))
        for d in (2, 6, 1, 7, 0):
            part_copy(d).wait()

    def ring_step(k, second):
        for i in range(3):
            for sign in (1, -1):
                p = later(sign if second else -sign)[i]
                ring(sign, k, p).wait_recv()
                spot = p % 3 if k == 1 else 6 * k - 9 + p
                add(parts.at[(sign * (4 - k)) % REPLICAS, p], ring_in.at[(1 - sign) // 2, spot])
                start(ring(sign, k + 1, p))

    def hand_over(i):
        return remote(
            parts.at[0, 3 * i + 2], copy_in.at[i], send_c.at[i], recv_c.at[i], place.before())

    def ring_end(p):
        for sign in (1, -1):
            ring(sign, 4, p).wait_recv()
        spot = 15 + p
        if p % 3 == 2:
            add(parts.at[0, p], ring_in.at[0, spot], ring_in.at[1, spot])
            start(hand_over(p // 3))
            return None
        total = parts[0, p].astype(F32)
        for way in range(2):
            total = total + ring_in[way, spot].astype(F32)
        if p % 3 == 0:
            hand_over(p // 3).wait_recv()
            total = total + copy_in[p // 3].astype(F32)
        return total

    def ring_result(i, result):
        cold = ring_end(3 * i + 1)
        hot = ring_end(3 * i)
        hot_first = first_ref[:1, :1] > 0.5
        for e, value in enumerate((jnp.where(hot_first, hot, cold), jnp.where(hot_first, cold, hot))):
            result[e] = (jnp.transpose(value) if i == 0 else value).astype(BF)

    def unit_copies(slot, a, r):
        first, count = SPANS[r]
        b = (place.b + slot) % SIDE
        return pltpu.make_async_copy(
            ins[a][r].at[place.core * SIDE + b], rows.at[slot, a, pl.ds(first, count)],
            in_sem.at[slot, a, r])

    def unit_sends(slot, a, r):
        first, count = SPANS[r]
        b = (place.s + slot) % SIDE
        return remote(
            ins[a][r].at[(1 - place.core) * SIDE + b],
            rows.at[slot, a, pl.ds(UNIT + first, count)],
            send_r.at[slot, a, r], recv_r.at[slot, a, r], place.partner())

    def chunk(slot, a, ds, part=None):
        s = (place.s + ds + SIDE) % SIDE
        first = pl.multiple_of(s * rows_of, rows_of)
        if part is None:
            return sums.at[slot, a, pl.ds(first, rows_of)]
        return sums.at[slot, a, pl.ds(pl.multiple_of(first + part * half, half), half)]

    def far(slot, a, sign):
        part = (1 - sign) // 2
        return remote(
            chunk(slot, a, 2, part), first_in.at[slot, a, part],
            send_1.at[slot, a, part], recv_1.at[slot, a, part], place.at(0, sign))

    def near(slot, a, sign, part):
        way = (1 - sign) // 2
        return remote(
            chunk(slot, a, sign, part), second_in.at[slot, a, way, pl.ds(part * half, half)],
            send_2.at[slot, a, way, part], recv_2.at[slot, a, way, part],
            place.at(0, sign))

    def far_b(a, sign):
        part = (1 - sign) // 2
        return remote(
            chunk(2, a, 0, part), third_in.at[a, part],
            send_3.at[a, part], recv_3.at[a, part], place.at(sign, 0))

    def near_b(a, sign, part):
        way = (1 - sign) // 2
        return remote(
            chunk(sign % SIDE, a, 0, part), fourth_in.at[a, way, pl.ds(part * half, half)],
            send_4.at[a, way, part], recv_4.at[a, way, part], place.at(sign, 0))

    def add(into, *others):
        @pl.loop(0, into.shape[0] // 32)
        def _(i):
            span = pl.ds(pl.multiple_of(i * 32, 32), 32)
            total = into[span].astype(F32)
            for other in others:
                total = total + other[span].astype(F32)
            into[span] = total.astype(BF)

    for slot in order:
        for a in range(2):
            for r in range(3):
                start(unit_sends(slot, a, r))
                unit_copies(slot, a, r).start()

    def spread_copy(slot):
        b = (place.b + slot) % SIDE
        turn = order.index(slot) % 2
        return pltpu.make_async_copy(spread_ref.at[b], spread.at[turn], spread_sem.at[slot])

    for slot in order[:2]:
        spread_copy(slot).start()

    def expand(slot):
        turn = order.index(slot)
        spread_copy(slot).wait()
        for a in range(2):
            for r in range(3):
                unit_copies(slot, a, r).wait()
                unit_sends(slot, a, r).wait_recv()

            @pl.loop(0, width // 512)
            def _(j):
                cols = pl.ds(pl.multiple_of(j * 512, 512), 512)
                own = jnp.dot(
                    spread[turn % 2, 0], rows[slot, a, pl.ds(0, UNIT), cols],
                    preferred_element_type=F32)
                other = jnp.dot(
                    spread[turn % 2, 1], rows[slot, a, pl.ds(UNIT, UNIT), cols],
                    preferred_element_type=F32)
                sums[slot, a, :, cols] = (own + other).astype(BF)

            for sign in (1, -1):
                start(far(slot, a, sign))
            for sign in (1, -1):
                start(near(slot, a, sign, (1 + sign) // 2))
        if turn < 2:
            spread_copy(order[turn + 2]).start()

    def pass_on(slot):
        for a in range(2):
            for sign in (1, -1):
                part = (1 - sign) // 2
                far(slot, a, sign).wait_recv()
                add(chunk(slot, a, sign, part), first_in.at[slot, a, part])
                start(near(slot, a, sign, part))

    def finish(slot):
        for a in range(2):
            for sign in (1, -1):
                for part in range(2):
                    near(slot, a, sign, part).wait_recv()
            add(chunk(slot, a, 0), second_in.at[slot, a, 0], second_in.at[slot, a, 1])

    ring_start()
    expand(2)
    expand(3)
    pass_on(2)
    ring_step(1, True)
    expand(1)
    ring_step(2, False)
    pass_on(3)
    finish(2)
    for a in range(2):
        for sign in (1, -1):
            start(far_b(a, sign))
    expand(0)
    ring_step(2, True)
    pass_on(1)
    finish(3)
    for a in range(2):
        start(near_b(a, -1, 0))
    ring_step(3, False)
    pass_on(0)
    finish(1)
    for a in range(2):
        start(near_b(a, 1, 1))
    ring_step(3, True)
    for a in range(2):
        for sign in (1, -1):
            part = (1 - sign) // 2
            far_b(a, sign).wait_recv()
            add(chunk(sign % SIDE, a, 0, part), third_in.at[a, part])
            start(near_b(a, sign, part))
    finish(0)
    for p in (5, 2):
        ring_end(p)
    for a, result in ((0, out_ref), (1, grad_ref)):
        for sign in (1, -1):
            for part in range(2):
                near_b(a, sign, part).wait_recv()
        own = chunk(0, a, 0)
        result[...] = (
            own[...].astype(F32) + fourth_in[a, 0].astype(F32) + fourth_in[a, 1].astype(F32)
        ).astype(BF)
    ring_result(1, down_ref)
    ring_result(0, up_ref)
    for copy in started:
        copy.wait_send()


def scatter_rows(out_rows, grad_rows, spread, grads, hot_first, rows_of):
    width = out_rows[0].shape[-1]
    hidden = grads.shape[1]
    piece = width // REPLICAS
    half = rows_of // 2
    anywhere = pl.BlockSpec(memory_space=pl.ANY)
    vmem = pl.BlockSpec(memory_space=pltpu.VMEM)
    shape = jax.ShapeDtypeStruct((rows_of, width), BF)
    dma = pltpu.SemaphoreType.DMA
    return pl.pallas_call(
        scatter_kernel,
        out_shape=(
            shape, shape, jax.ShapeDtypeStruct((2, piece, hidden), BF),
            jax.ShapeDtypeStruct((2, hidden, piece), BF),
        ),
        in_specs=[anywhere] * 8 + [vmem],
        out_specs=(vmem,) * 4,
        scratch_shapes=[
            pltpu.VMEM((SIDE, 2, 2 * UNIT, width), BF),
            pltpu.VMEM((SIDE, 2, SIDE * rows_of, width), BF),
            pltpu.VMEM((SIDE, 2, 2, half, width), BF),
            pltpu.VMEM((SIDE, 2, 2, rows_of, width), BF),
            pltpu.VMEM((2, 2, half, width), BF),
            pltpu.VMEM((2, 2, rows_of, width), BF),
            pltpu.VMEM((REPLICAS, 6, hidden, piece), BF),
            pltpu.VMEM((2, 21, hidden, piece), BF),
            pltpu.VMEM((2, hidden, piece), BF),
            pltpu.VMEM((2, 2, SIDE * rows_of, UNIT), BF),
            dma((SIDE, 2, 3)),
            dma((SIDE, 2, 3)),
            dma((SIDE, 2, 3)),
            dma((SIDE, 2, 2)),
            dma((SIDE, 2, 2)),
            dma((SIDE, 2, 2, 2)),
            dma((SIDE, 2, 2, 2)),
            dma((2, 2)),
            dma((2, 2)),
            dma((2, 2, 2)),
            dma((2, 2, 2)),
            dma((REPLICAS,)),
            dma((2, 21)),
            dma((2, 21)),
            dma((2,)),
            dma((2,)),
            dma((SIDE,)),
        ],
        compiler_params=pltpu.CompilerParams(
            collective_id=1, has_side_effects=True, vmem_limit_bytes=67043328
        ),
        name="scatter_rows",
    )(*out_rows, *grad_rows, spread, grads, hot_first)


def local(
    tokens,
    cotangent,
    gate_weights,
    expert_ids,
    copy_pick,
    copy_expert,
    up_weight,
    down_weight,
    copy_up,
    copy_down,
):
    me = lax.axis_index("expert")
    rows_of, width = tokens.shape
    table, dest, slot = route(expert_ids.T, copy_pick.T, gate_weights.T, copy_expert)
    *gathered, gates, spread = gather_rows(tokens, cotangent, table)
    *rows, grads, back = serve(
        copy_expert,
        [part.reshape(-1, width) for part in gathered],
        gates, up_weight, down_weight, copy_up, copy_down,
    )
    rows = [part.reshape(2 * SIDE, -1, width) for part in rows]
    hot_first = copy_expert[(me + 1) % DEVICES] % 2 == 0
    hot_first = jnp.broadcast_to(hot_first.astype(F32), (8, 128))
    layer_output, token_grad, up_grad, down_grad = scatter_rows(
        rows[:3], rows[3:], spread, grads, hot_first, rows_of
    )
    returned = lax.all_to_all(back, "expert", split_axis=0, concat_axis=0, tiled=True)
    gate_grad = gate_back(dest, slot, returned).T
    return layer_output, token_grad, gate_grad, up_grad, down_grad


def solution(mesh):
    rows = P(("expert", "dp"), None)
    held = P("expert", None, None)
    return jax.shard_map(
        local,
        mesh=mesh,
        in_specs=(rows,) * 5 + (P(),) + (held,) * 4,
        out_specs=(rows, rows, rows, P("expert", "dp", None), P("expert", None, "dp")),
        check_vma=False,
    )
```

```python
import functools

import jax
import jax.numpy as jnp
from jax import lax
from jax.experimental import pallas as pl
from jax.experimental.pallas import tpu as pltpu
from jax.sharding import PartitionSpec as P

SIDE = 4
HOT, COLD, COPY = 24, 12, 6
SLOTS = 48
REPLICAS = 8
DEVICES = 2 * SIDE * SIDE
HOT_U, COLD_U, COPY_U = SIDE * HOT, SIDE * COLD, 32
UNIT = HOT_U + COLD_U + COPY_U
SPANS = ((0, HOT_U), (HOT_U, COLD_U), (HOT_U + COLD_U, COPY_U))
BF = jnp.bfloat16
F32 = jnp.float32
EXACT = lax.Precision.HIGHEST


def iota(shape, dim):
    return lax.broadcasted_iota(jnp.int32, shape, dim)


def route_kernel(ids_ref, picks_ref, gates_ref, listed_ref, table_ref):
    chosen, rows = ids_ref.shape
    ids, picks, gates = ids_ref[...], picks_ref[...], gates_ref[...]
    devices = listed_ref.shape[0]
    cold = jnp.ones((chosen, rows), jnp.int32)
    for i in range(devices):
        cold = jnp.where(ids == listed_ref[i], 0, cold)
    before = (iota((rows, rows), 0) < iota((rows, rows), 1)).astype(BF)
    lines = iota((128, rows), 0)
    token = iota((128, rows), 1).astype(F32) + 1.0
    offset = jnp.zeros((128, 1), F32)
    table = jnp.zeros((devices, 128), F32)
    for k in range(chosen):
        e, p, g = ids[k : k + 1], picks[k : k + 1], gates[k : k + 1]
        dest = (e // 2 + p) % devices
        region = jnp.where(p == 1, 2, cold[k : k + 1])
        hit = (region * devices + dest == lines).astype(F32)
        ahead = jnp.dot(hit.astype(BF), before, preferred_element_type=F32) + offset
        rank = jnp.sum(hit * ahead, axis=0, keepdims=True).astype(jnp.int32)
        offset = offset + jnp.sum(hit, axis=1, keepdims=True)
        base = jnp.where(region == 0, 0, jnp.where(region == 1, HOT, HOT + COLD))
        slot = base + rank
        to = (dest == iota((devices, rows), 0)).astype(F32)
        code = token + float(k * rows)
        value = jnp.where(slot == lines, code, 0.0) + jnp.where(slot + 64 == lines, g, 0.0)
        table = table + across(to, value, EXACT)
    table_ref[...] = table


def across(a, b, precision=None):
    return lax.dot_general(
        a, b, (((1,), (1,)), ((), ())), precision=precision, preferred_element_type=F32
    )


def route(ids, picks, gates, listed):
    vmem = pl.BlockSpec(memory_space=pltpu.VMEM)
    return pl.pallas_call(
        route_kernel,
        out_shape=jax.ShapeDtypeStruct((listed.shape[0], 128), F32),
        in_specs=[vmem] * 3 + [pl.BlockSpec(memory_space=pltpu.SMEM)],
        out_specs=vmem,
        name="route",
    )(ids, picks, gates, listed)


def seats(s, rows, lead):
    row, lane = iota((rows, 128), 0), iota((rows, 128), 1) - lead
    hot = (row - HOT * s == lane) & (lane >= 0) & (lane < HOT)
    cold = (row - HOT_U - COLD * s == lane - HOT) & (lane >= HOT) & (lane < HOT + COLD)
    copied = (row - HOT_U - COLD_U - COPY * s == lane - HOT - COLD) & (lane >= HOT + COLD)
    copied = copied & (lane < HOT + COLD + COPY)
    return (hot | cold | copied).astype(F32)


def finish_kernel(count, *refs):
    ins, outs, held, sems = refs[:count], refs[count : 2 * count], refs[2 * count : -1], refs[-1]
    loads = [pltpu.make_async_copy(ins[i], held[i], sems.at[0, i]) for i in range(count)]
    stores = [pltpu.make_async_copy(held[i], outs[i], sems.at[1, i]) for i in range(count)]
    for load in loads:
        load.start()
    for load, store in zip(loads, stores):
        load.wait()
        store.start()
    for store in stores:
        store.wait()


def finish(*arrays):
    anywhere = pl.BlockSpec(memory_space=pl.ANY)
    count = len(arrays)
    return pl.pallas_call(
        functools.partial(finish_kernel, count),
        out_shape=tuple(jax.ShapeDtypeStruct(x.shape, x.dtype) for x in arrays),
        in_specs=[anywhere] * count,
        out_specs=(anywhere,) * count,
        scratch_shapes=[pltpu.VMEM(x.shape, x.dtype) for x in arrays]
        + [pltpu.SemaphoreType.DMA((2, count))],
        name="finish",
    )(*arrays)


def serve_kernel(
    which_ref, hot_t, cold_t, copy_t, hot_c, cold_c, copy_c, gates_ref, up_ref, down_ref,
    copy_up_ref, copy_down_ref, hot_o, cold_o, copy_o, hot_g, cold_g, copy_g, grads_ref, back_ref,
    x, c, u, v, o, q, w, linear, slope, active, sums, gate_cols, by_unit, in_sem, out_sem,
):
    firsts = (0, hot_t.shape[0], hot_t.shape[0] + cold_t.shape[0])
    counts = (hot_t.shape[0], cold_t.shape[0], copy_t.shape[0])
    width = x.shape[1]
    step = 1024
    me = lax.axis_index("expert")
    hot = which_ref[(me + 1) % DEVICES] % 2
    ups = (up_ref.at[hot], up_ref.at[1 - hot], copy_up_ref.at[0])
    downs = (down_ref.at[hot], down_ref.at[1 - hot], copy_down_ref.at[0])

    def loads(r):
        span = pl.ds(firsts[r], counts[r])
        pairs = (
            ((hot_t, cold_t, copy_t)[r], x.at[span]),
            (ups[r], u.at[r]),
            (downs[r], v.at[r]),
            ((hot_c, cold_c, copy_c)[r], c.at[span]),
        )
        return [pltpu.make_async_copy(*pair, in_sem.at[r, i]) for i, pair in enumerate(pairs)]

    stores = []

    def store(src, dst, r, i):
        copy = pltpu.make_async_copy(src, dst, out_sem.at[r, i])
        copy.start()
        stores.append(copy)

    for r in (2, 1, 0):
        for copy in loads(r):
            copy.start()
    for i in range(2 * SIDE):
        columns = jnp.transpose(jnp.broadcast_to(gates_ref[i, :1], (128, gates_ref.shape[2])))
        for r, (low, rows) in enumerate(SPANS):
            gate_cols[pl.ds(firsts[r] + i * rows, rows)] = columns[low : low + rows]
    by_unit[...] = jnp.zeros_like(by_unit)
    for r in (2, 1, 0):
        first, count = firsts[r], counts[r]
        span = pl.ds(first, count)
        ready = loads(r)
        gate = gate_cols[span][:, :1]
        ready[0].wait()
        ready[1].wait()
        tile = count

        @pl.loop(0, count // tile)
        def _(i):
            rows = pl.ds(pl.multiple_of(i * tile, tile), tile)
            value = jnp.dot(
                x[pl.ds(pl.multiple_of(first + i * tile, 128), tile)], u[r],
                preferred_element_type=F32)
            sigma = 1.0 / (1.0 + jnp.exp(-value))
            slope[rows] = sigma * (1.0 + value * (1.0 - sigma))
            active[rows] = (value * sigma).astype(BF)
            linear[rows] = value * sigma

        sums[pl.ds(0, count)] = jnp.zeros((count, 128), F32)
        ready[2].wait()
        ready[3].wait()

        @pl.loop(0, width // step)
        def _(j):
            cols = pl.ds(pl.multiple_of(j * step, step), step)
            served = jnp.dot(
                active[pl.ds(0, count)], v[r, :, cols], preferred_element_type=F32
            )
            cot = c[span, cols].astype(F32)
            both = served * cot
            part = both[:, :128]
            for i in range(1, step // 128):
                part = part + both[:, i * 128 : (i + 1) * 128]
            sums[pl.ds(0, count)] += part
            o[span, cols] = (gate * served).astype(BF)
            c[span, cols] = (gate * cot).astype(BF)

        store(o.at[span], (hot_o, cold_o, copy_o)[r], r, 0)

        @pl.loop(0, count // tile)
        def _(i):
            rows = pl.ds(pl.multiple_of(i * tile, tile), tile)
            value = across(c[pl.ds(pl.multiple_of(first + i * tile, 128), tile)], v[r])
            slope[rows] = value * slope[rows]

        low, rows = SPANS[r]
        totals = jnp.zeros((rows, 128), F32)
        for i in range(2 * SIDE):
            one = jnp.sum(sums[pl.ds(i * rows, rows)], axis=1, keepdims=True)
            totals = jnp.where(iota((rows, 128), 1) == i, one, totals)
        by_unit[pl.ds(low, rows)] = totals
        slanted = slope[pl.ds(0, count)]
        linear_grad = slanted.astype(BF)
        turned = jnp.transpose(slanted).astype(BF)
        active_turned = jnp.transpose(linear[pl.ds(0, count)]).astype(BF)

        @pl.loop(0, width // step)
        def _(j):
            cols = pl.ds(pl.multiple_of(j * step, step), step)
            q[span, cols] = across(linear_grad, u[r, cols]).astype(BF)
            w[r, :, cols] = jnp.dot(turned, x[span, cols], preferred_element_type=F32).astype(BF)
            w[3 + r, :, cols] = jnp.dot(
                active_turned, c[span, cols], preferred_element_type=F32
            ).astype(BF)

        store(q.at[span], (hot_g, cold_g, copy_g)[r], r, 1)
        store(w.at[r], grads_ref.at[r], r, 2)
        store(w.at[3 + r], grads_ref.at[3 + r], r, 3)
    turned = jnp.transpose(by_unit[...])
    for i in range(2 * SIDE):
        back_ref[i] = jnp.broadcast_to(turned[i : i + 1], back_ref.shape[1:])
    for copy in stores:
        copy.wait()


def serve(listed, gathered, gates, up_weight, down_weight, copy_up, copy_down):
    width, hidden = up_weight.shape[1:]
    counts = [rows.shape[0] for rows in gathered[:3]]
    total = sum(counts)
    anywhere = pl.BlockSpec(memory_space=pl.ANY)
    vmem = pl.BlockSpec(memory_space=pltpu.VMEM)
    rows = [jax.ShapeDtypeStruct((count, width), BF) for count in counts]
    return pl.pallas_call(
        serve_kernel,
        out_shape=(
            *rows, *rows, jax.ShapeDtypeStruct((6, hidden, width), BF),
            jax.ShapeDtypeStruct((2 * SIDE, 8, 256), F32),
        ),
        in_specs=[pl.BlockSpec(memory_space=pltpu.SMEM)] + [anywhere] * 6 + [vmem] + [anywhere] * 4,
        out_specs=(anywhere,) * 7 + (vmem,),
        scratch_shapes=[
            pltpu.VMEM((total, width), BF),
            pltpu.VMEM((total, width), BF),
            pltpu.VMEM((3, width, hidden), BF),
            pltpu.VMEM((3, hidden, width), BF),
            pltpu.VMEM((total, width), BF),
            pltpu.VMEM((total, width), BF),
            pltpu.VMEM((6, hidden, width), BF),
            pltpu.VMEM((counts[0], hidden), F32),
            pltpu.VMEM((counts[0], hidden), F32),
            pltpu.VMEM((counts[0], hidden), BF),
            pltpu.VMEM((counts[0], 128), F32),
            pltpu.VMEM((total, 128), F32),
            pltpu.VMEM((256, 128), F32),
            pltpu.SemaphoreType.DMA((3, 4)),
            pltpu.SemaphoreType.DMA((3, 4)),
        ],
        compiler_params=pltpu.CompilerParams(vmem_limit_bytes=62 << 20),
        name="serve",
    )(listed, *gathered, gates, up_weight, down_weight, copy_up, copy_down)


class Place:
    def __init__(self):
        me = lax.axis_index("expert")
        self.me = me
        self.core = me % 2
        x = (me // 2) % SIDE
        y = me // (2 * SIDE)
        self.s = x * (1 - self.core) + y * self.core
        self.b = y * (1 - self.core) + x * self.core

    def at(self, db, ds):
        b = (self.b + db + SIDE) % SIDE
        s = (self.s + ds + SIDE) % SIDE
        y = b * (1 - self.core) + s * self.core
        x = s * (1 - self.core) + b * self.core
        return {"expert": (y * SIDE + x) * 2 + self.core}

    def partner(self):
        return {"expert": self.me + 1 - 2 * self.core}

    def replica(self, dz):
        return {"dp": (lax.axis_index("dp") + dz + REPLICAS) % REPLICAS}

    def before(self):
        return {"expert": (self.me + DEVICES - 1) % DEVICES}

    def beyond(self):
        return {"expert": (self.me + DEVICES - 1 + 2 * self.core) % DEVICES}


def greet(place, *more):
    barrier = pltpu.get_barrier_semaphore()
    others = [place.at(0, 1), place.at(0, -1), place.at(1, 0), place.at(-1, 0), place.partner()]
    others.extend(more)
    for other in others:
        pl.semaphore_signal(barrier, inc=1, device_id=other, device_id_type=pl.DeviceIdType.MESH)
    pl.semaphore_wait(barrier, len(others))


def remote(src, dst, send, recv, device):
    return pltpu.make_async_remote_copy(
        src_ref=src,
        dst_ref=dst,
        send_sem=send,
        recv_sem=recv,
        device_id=device,
        device_id_type=pl.DeviceIdType.MESH,
    )


def gather_kernel(
    tok_ref, cot_ref, table_ref, hot_t, cold_t, copy_t, hot_c, cold_c, copy_c, gates_ref, spread_ref, kinds_ref,
    held, tables, rows, picks, spread, gates, kinds, own_sem, send, recv, out_sem, gate_sem, spread_sem,
):
    place = Place()
    rows_of = tok_ref.shape[0]
    width = tok_ref.shape[1]
    sources = (tok_ref, cot_ref, table_ref)
    outs = ((hot_t, cold_t, copy_t), (hot_c, cold_c, copy_c))
    started = []
    greet(place)

    def start(copy):
        copy.start()
        started.append(copy)
        return copy

    def spot(a, db, ds, part=None):
        b = (place.b + db + SIDE) % SIDE
        s = (place.s + ds + SIDE) % SIDE
        count = sources[a].shape[0]
        half = count // 2
        first = pl.multiple_of(s * count, count)
        within = tables.at[b] if a == 2 else held.at[a, b]
        if part is None:
            return within.at[pl.ds(first, count)]
        return within.at[pl.ds(pl.multiple_of(first + part * half, half), half)]

    def full_s(a, sign):
        return remote(
            sources[a], spot(a, 0, 0), send.at[0, 0, (1 - sign) // 2, a, 0],
            recv.at[0, 0, (1 - sign) // 2, a, 0], place.at(0, sign))

    def half_s(a, sign):
        part = (1 - sign) // 2
        return remote(
            spot(a, 0, -sign, part), spot(a, 0, -sign, part), send.at[1, 0, part, a, 0],
            recv.at[1, 0, part, a, 0], place.at(0, sign))

    def full_b(a, sign, ds):
        src = sources[a] if ds == 0 else spot(a, 0, ds)
        return remote(
            src, spot(a, 0, ds), send.at[0, 1, (1 - sign) // 2, a, ds % SIDE],
            recv.at[0, 1, (1 - sign) // 2, a, ds % SIDE], place.at(sign, 0))

    def half_b(a, sign, ds):
        part = (1 - sign) // 2
        return remote(
            spot(a, -sign, ds, part), spot(a, -sign, ds, part),
            send.at[1, 1, part, a, ds % SIDE], recv.at[1, 1, part, a, ds % SIDE],
            place.at(sign, 0))

    def plan(db):
        b = (place.b + db + SIDE) % SIDE
        slot = db % SIDE
        for h in range(2):
            target = place.me + h * (1 - 2 * place.core)
            scale = jnp.zeros((8, UNIT), F32)
            kind = jnp.zeros((8, UNIT), F32)
            for s in range(SIDE):
                line = tables[b, pl.ds(s * DEVICES + target, 1), :]
                wide = jnp.broadcast_to(line, (128, 128))
                code = wide.astype(jnp.int32) - 1
                token = jnp.where(code >= 0, code % 128, -1)
                one = (jnp.transpose(token.astype(F32)) == iota((128, 128), 1).astype(F32)).astype(BF)
                turned = (token == iota((128, 128), 0)).astype(BF)
                seat = seats(s, UNIT, 0).astype(BF)
                span = pl.ds(s * rows_of, rows_of)
                picks[slot, h, :, span] = jnp.dot(seat, one, preferred_element_type=F32).astype(BF)
                spread[slot, h, span, :] = across(turned, seat).astype(BF)
                scale = scale + across(wide[:8], seats(s, UNIT, 64), EXACT)
                kind = kind + across((code[:8] // 128).astype(F32).astype(BF), seat)
            gates[slot, h, :, pl.ds(0, UNIT)] = scale
            kinds[slot, h, :, pl.ds(0, UNIT)] = kind
        unit = place.core * SIDE + b
        keep(pltpu.make_async_copy(gates.at[slot, 0], gates_ref.at[unit], gate_sem.at[0, slot]))
        start(gates_out(slot))
        keep(pltpu.make_async_copy(spread.at[slot], spread_ref.at[b], spread_sem.at[0, slot]))
        keep(pltpu.make_async_copy(kinds.at[slot], kinds_ref.at[b], spread_sem.at[1, slot]))

    def gates_out(slot):
        b = (place.b + slot) % SIDE
        return remote(
            gates.at[slot, 1], gates_ref.at[place.core * SIDE + b], gate_sem.at[1, slot],
            gate_sem.at[2, slot], place.partner())

    def rows_out(slot, a, r):
        b = (place.b + slot) % SIDE
        first, count = SPANS[r]
        return remote(
            rows.at[slot, a, 1, pl.ds(first, count)], outs[a][r].at[place.core * SIDE + b],
            out_sem.at[1, slot, a, r], out_sem.at[2, slot, a, r], place.partner())

    def pick(db, a):
        b = (place.b + db + SIDE) % SIDE
        slot = db % SIDE
        for h in (1, 0):

            @pl.loop(0, width // 512)
            def _(j):
                cols = pl.ds(pl.multiple_of(j * 512, 512), 512)
                rows[slot, a, h, :, cols] = jnp.dot(
                    picks[slot, h], held[a, b, :, cols], preferred_element_type=F32
                ).astype(BF)

            for r, (first, count) in enumerate(SPANS):
                if h == 1:
                    start(rows_out(slot, a, r))
                else:
                    keep(
                        pltpu.make_async_copy(
                            rows.at[slot, a, 0, pl.ds(first, count)],
                            outs[a][r].at[place.core * SIDE + b], out_sem.at[0, slot, a, r]))

    kept = []

    def keep(copy):
        copy.start()
        kept.append(copy)

    gates[...] = jnp.zeros_like(gates)
    kinds[...] = jnp.zeros_like(kinds)
    arrays = (2, 0, 1)
    for a in arrays:
        for sign in (1, -1):
            start(full_s(a, sign))
        for sign in (1, -1):
            start(full_b(a, sign, 0))
    for a in arrays:
        keep(pltpu.make_async_copy(sources[a], spot(a, 0, 0), own_sem.at[a]))
    for a in arrays:
        for sign in (1, -1):
            full_s(a, sign).wait_recv()
            start(half_s(a, sign))
            for way in (1, -1):
                start(full_b(a, way, -sign))
        for sign in (1, -1):
            full_b(a, sign, 0).wait_recv()
            start(half_b(a, sign, 0))
    for a in arrays:
        for sign in (1, -1):
            half_s(a, sign).wait_recv()
        for way in (1, -1):
            start(full_b(a, way, 2))
    for copy in kept:
        copy.wait()
    kept.clear()
    plan(0)
    for a in range(2):
        pick(0, a)
    for ds in (-1, 1, 2):
        for a in arrays:
            for sign in (1, -1):
                full_b(a, sign, ds).wait_recv()
                start(half_b(a, sign, ds))
    for db in (1, -1):
        plan(db)
        for a in range(2):
            pick(db, a)
    for ds in (0, -1, 1, 2):
        for sign in (1, -1):
            half_b(2, sign, ds).wait_recv()
    plan(2)
    for a in range(2):
        for ds in (0, -1, 1, 2):
            for sign in (1, -1):
                half_b(a, sign, ds).wait_recv()
        pick(2, a)
    for copy in kept:
        copy.wait()
    for slot in range(SIDE):
        gates_out(slot).wait_recv()
        for a in range(2):
            for r in range(3):
                rows_out(slot, a, r).wait_recv()
    for copy in started:
        copy.wait_send()


def gather_rows(tokens, cotangent, table):
    width = tokens.shape[1]
    rows_of = tokens.shape[0]
    shapes = [jax.ShapeDtypeStruct((2 * SIDE, count, width), BF) for _, count in SPANS]
    dma = pltpu.SemaphoreType.DMA
    anywhere = pl.BlockSpec(memory_space=pl.ANY)
    return pl.pallas_call(
        gather_kernel,
        out_shape=(
            *shapes, *shapes, jax.ShapeDtypeStruct((2 * SIDE, 8, 256), F32),
            jax.ShapeDtypeStruct((SIDE, 2, SIDE * rows_of, UNIT), BF),
            jax.ShapeDtypeStruct((SIDE, 2, 8, 256), F32),
        ),
        in_specs=[anywhere] * 3,
        out_specs=(anywhere,) * 9,
        scratch_shapes=[
            pltpu.VMEM((2, SIDE, SIDE * rows_of, width), BF),
            pltpu.VMEM((SIDE, SIDE * DEVICES, 128), F32),
            pltpu.VMEM((SIDE, 2, 2, UNIT, width), BF),
            pltpu.VMEM((SIDE, 2, UNIT, SIDE * rows_of), BF),
            pltpu.VMEM((SIDE, 2, SIDE * rows_of, UNIT), BF),
            pltpu.VMEM((SIDE, 2, 8, 256), F32),
            pltpu.VMEM((SIDE, 2, 8, 256), F32),
            dma((3,)),
            dma((2, 2, 2, 3, SIDE)),
            dma((2, 2, 2, 3, SIDE)),
            dma((3, SIDE, 2, 3)),
            dma((3, SIDE)),
            dma((2, SIDE)),
        ],
        compiler_params=pltpu.CompilerParams(
            collective_id=0, has_side_effects=True, vmem_limit_bytes=60 << 20
        ),
        name="gather_rows",
    )(tokens, cotangent, table)


def scatter_kernel(
    hot_o, cold_o, copy_o, hot_g, cold_g, copy_g, spread_ref, grads_ref, back_ref, kinds_ref, first_ref,
    out_ref, grad_ref, gate_ref, up_ref, down_ref,
    rows, sums, first_in, second_in, third_in, fourth_in,
    backs, kinds, gate_sums, gate_first, gate_second, gate_third, gate_fourth, parts, ring_in, copy_in, spread,
    in_sem, send_r, recv_r, send_1, recv_1, send_2, recv_2, send_3, recv_3, send_4, recv_4,
    part_sem, send_z, recv_z, send_c, recv_c, spread_sem, back_sem,
):
    place = Place()
    width = out_ref.shape[1]
    rows_of = out_ref.shape[0]
    arrays = (2, 0, 1)
    ins = ((hot_o, cold_o, copy_o), (hot_g, cold_g, copy_g))
    order = (2, 3, 1, 0)
    started = []
    greet(place, place.replica(1), place.replica(-1), place.beyond())

    def start(copy):
        copy.start()
        started.append(copy)

    def part_copy(d):
        z = (lax.axis_index("dp") + d) % REPLICAS
        piece = parts.shape[-1]
        return pltpu.make_async_copy(
            grads_ref.at[:, :, pl.ds(pl.multiple_of(z * piece, piece), piece)], parts.at[d],
            part_sem.at[d])

    def ring(sign, k, p):
        way = (1 - sign) // 2
        spot = p % 3 if k == 1 else 6 * k - 9 + p
        return remote(
            parts.at[(sign * (5 - k)) % REPLICAS, p], ring_in.at[way, spot],
            send_z.at[way, spot], recv_z.at[way, spot], place.replica(sign))

    def later(sign):
        return (2, 0, 1) if sign == 1 else (5, 3, 4)

    def ring_start():
        for d in (4, 3, 5, 2, 6, 1, 7, 0):
            part_copy(d).start()
        part_copy(4).wait()
        for i in range(3):
            for sign in (1, -1):
                start(ring(sign, 1, later(sign)[i]))
        part_copy(3).wait()
        part_copy(5).wait()
        for i in range(3):
            for sign in (1, -1):
                start(ring(sign, 2, later(-sign)[i]))
        for d in (2, 6, 1, 7, 0):
            part_copy(d).wait()

    def ring_step(k, second):
        for i in range(3):
            for sign in (1, -1):
                p = later(sign if second else -sign)[i]
                ring(sign, k, p).wait_recv()
                spot = p % 3 if k == 1 else 6 * k - 9 + p
                add(parts.at[(sign * (4 - k)) % REPLICAS, p], ring_in.at[(1 - sign) // 2, spot])
                start(ring(sign, k + 1, p))

    def hand_over(i):
        return remote(
            parts.at[0, 3 * i + 2], copy_in.at[i], send_c.at[i], recv_c.at[i], place.before())

    def ring_end(p):
        for sign in (1, -1):
            ring(sign, 4, p).wait_recv()
        spot = 15 + p
        if p % 3 == 2:
            add(parts.at[0, p], ring_in.at[0, spot], ring_in.at[1, spot])
            start(hand_over(p // 3))
            return None
        total = parts[0, p].astype(F32)
        for way in range(2):
            total = total + ring_in[way, spot].astype(F32)
        if p % 3 == 0:
            hand_over(p // 3).wait_recv()
            total = total + copy_in[p // 3].astype(F32)
        return total

    def ring_result(i, result):
        cold = ring_end(3 * i + 1)
        hot = ring_end(3 * i)
        hot_first = first_ref[:1, :1] > 0.5
        for e, value in enumerate((jnp.where(hot_first, hot, cold), jnp.where(hot_first, cold, hot))):
            result[e] = (jnp.transpose(value) if i == 0 else value).astype(BF)

    def unit_copies(slot, a, r):
        first, count = SPANS[r]
        b = (place.b + slot) % SIDE
        return pltpu.make_async_copy(
            ins[a][r].at[place.core * SIDE + b], rows.at[slot, a, pl.ds(first, count)],
            in_sem.at[slot, a, r])

    def unit_sends(slot, a, r):
        first, count = SPANS[r]
        b = (place.s + slot) % SIDE
        return remote(
            ins[a][r].at[(1 - place.core) * SIDE + b],
            rows.at[slot, a, pl.ds(UNIT + first, count)],
            send_r.at[slot, a, r], recv_r.at[slot, a, r], place.partner())

    def chunk(slot, a, ds, part=None):
        s = (place.s + ds + SIDE) % SIDE
        count = 16 if a == 2 else rows_of
        within = gate_sums.at[slot] if a == 2 else sums.at[slot, a]
        first = pl.multiple_of(s * count, count)
        if part is None:
            return within.at[pl.ds(first, count)]
        half = count // 2
        return within.at[pl.ds(pl.multiple_of(first + part * half, half), half)]

    def half_of(within, part):
        half = within.shape[0] // 2
        return within.at[pl.ds(part * half, half)]

    def first_at(slot, a, part):
        return gate_first.at[slot, part] if a == 2 else first_in.at[slot, a, part]

    def second_at(slot, a, way):
        return gate_second.at[slot, way] if a == 2 else second_in.at[slot, a, way]

    def third_at(a, part):
        return gate_third.at[part] if a == 2 else third_in.at[a, part]

    def fourth_at(a, way):
        return gate_fourth.at[way] if a == 2 else fourth_in.at[a, way]

    def far(slot, a, sign):
        part = (1 - sign) // 2
        return remote(
            chunk(slot, a, 2, part), first_at(slot, a, part),
            send_1.at[slot, a, part], recv_1.at[slot, a, part], place.at(0, sign))

    def near(slot, a, sign, part):
        way = (1 - sign) // 2
        return remote(
            chunk(slot, a, sign, part), half_of(second_at(slot, a, way), part),
            send_2.at[slot, a, way, part], recv_2.at[slot, a, way, part],
            place.at(0, sign))

    def far_b(a, sign):
        part = (1 - sign) // 2
        return remote(
            chunk(2, a, 0, part), third_at(a, part),
            send_3.at[a, part], recv_3.at[a, part], place.at(sign, 0))

    def near_b(a, sign, part):
        way = (1 - sign) // 2
        return remote(
            chunk(sign % SIDE, a, 0, part), half_of(fourth_at(a, way), part),
            send_4.at[a, way, part], recv_4.at[a, way, part], place.at(sign, 0))

    def add(into, *others):
        step = min(32, into.shape[0])

        @pl.loop(0, into.shape[0] // step)
        def _(i):
            span = pl.ds(pl.multiple_of(i * step, step), step)
            total = into[span].astype(F32)
            for other in others:
                total = total + other[span].astype(F32)
            into[span] = total.astype(into.dtype)

    def back_copies(slot):
        b = (place.b + slot) % SIDE
        return (
            pltpu.make_async_copy(
                back_ref.at[place.core * SIDE + b], backs.at[slot, 0], back_sem.at[0, slot]),
            pltpu.make_async_copy(kinds_ref.at[b], kinds.at[slot], back_sem.at[1, slot]),
        )

    def back_send(slot):
        b = (place.s + slot) % SIDE
        return remote(
            back_ref.at[(1 - place.core) * SIDE + b], backs.at[slot, 1],
            back_sem.at[2, slot], back_sem.at[3, slot], place.partner())

    for slot in order:
        start(back_send(slot))
        for copy in back_copies(slot):
            copy.start()
        for a in range(2):
            for r in range(3):
                start(unit_sends(slot, a, r))
                unit_copies(slot, a, r).start()

    def spread_copy(slot):
        b = (place.b + slot) % SIDE
        turn = order.index(slot) % 2
        return pltpu.make_async_copy(spread_ref.at[b], spread.at[turn], spread_sem.at[slot])

    for slot in order[:2]:
        spread_copy(slot).start()

    def expand(slot):
        turn = order.index(slot)
        spread_copy(slot).wait()
        for copy in back_copies(slot):
            copy.wait()
        back_send(slot).wait_recv()
        gate = jnp.zeros((8, SIDE * rows_of), F32)
        for h in range(2):
            kind = kinds[slot, h, :, pl.ds(0, UNIT)]
            rest = backs[slot, h, :, pl.ds(0, UNIT)]
            rest = jnp.where(kind == iota((8, UNIT), 0).astype(F32), rest, 0.0)
            for _ in range(3):
                top = rest.astype(BF)
                rest = rest - top.astype(F32)
                gate = gate + across(top, spread[turn % 2, h])
        for s in range(SIDE):
            gate_sums[slot, pl.ds(16 * s, 8)] = gate[:, s * rows_of : (s + 1) * rows_of]
            gate_sums[slot, pl.ds(16 * s + 8, 8)] = jnp.zeros((8, rows_of), F32)
        for sign in (1, -1):
            start(far(slot, 2, sign))
        for sign in (1, -1):
            start(near(slot, 2, sign, (1 + sign) // 2))
        for a in range(2):
            for r in range(3):
                unit_copies(slot, a, r).wait()
                unit_sends(slot, a, r).wait_recv()

            @pl.loop(0, width // 512)
            def _(j):
                cols = pl.ds(pl.multiple_of(j * 512, 512), 512)
                own = jnp.dot(
                    spread[turn % 2, 0], rows[slot, a, pl.ds(0, UNIT), cols],
                    preferred_element_type=F32)
                other = jnp.dot(
                    spread[turn % 2, 1], rows[slot, a, pl.ds(UNIT, UNIT), cols],
                    preferred_element_type=F32)
                sums[slot, a, :, cols] = (own + other).astype(BF)

            for sign in (1, -1):
                start(far(slot, a, sign))
            for sign in (1, -1):
                start(near(slot, a, sign, (1 + sign) // 2))
        if turn < 2:
            spread_copy(order[turn + 2]).start()

    def pass_on(slot):
        for a in arrays:
            for sign in (1, -1):
                part = (1 - sign) // 2
                far(slot, a, sign).wait_recv()
                add(chunk(slot, a, sign, part), first_at(slot, a, part))
                start(near(slot, a, sign, part))

    def finish(slot):
        for a in arrays:
            for sign in (1, -1):
                for part in range(2):
                    near(slot, a, sign, part).wait_recv()
            add(chunk(slot, a, 0), second_at(slot, a, 0), second_at(slot, a, 1))

    ring_start()
    expand(2)
    expand(3)
    pass_on(2)
    ring_step(1, True)
    expand(1)
    ring_step(2, False)
    pass_on(3)
    finish(2)
    for a in arrays:
        for sign in (1, -1):
            start(far_b(a, sign))
    expand(0)
    ring_step(2, True)
    pass_on(1)
    finish(3)
    for a in arrays:
        start(near_b(a, -1, 0))
    ring_step(3, False)
    pass_on(0)
    finish(1)
    for a in arrays:
        start(near_b(a, 1, 1))
    ring_step(3, True)
    for a in arrays:
        for sign in (1, -1):
            part = (1 - sign) // 2
            far_b(a, sign).wait_recv()
            add(chunk(sign % SIDE, a, 0, part), third_at(a, part))
            start(near_b(a, sign, part))
    finish(0)
    for p in (5, 2):
        ring_end(p)
    for a in arrays:
        for sign in (1, -1):
            for part in range(2):
                near_b(a, sign, part).wait_recv()
        add(chunk(0, a, 0), fourth_at(a, 0), fourth_at(a, 1))
        if a == 2:
            gate_ref[...] = chunk(0, a, 0, 0)[...]
        else:
            (out_ref, grad_ref)[a][...] = chunk(0, a, 0)[...]
    ring_result(1, down_ref)
    ring_result(0, up_ref)
    for copy in started:
        copy.wait_send()


def scatter_rows(out_rows, grad_rows, spread, grads, back, kinds, hot_first, rows_of):
    width = out_rows[0].shape[-1]
    hidden = grads.shape[1]
    piece = width // REPLICAS
    half = rows_of // 2
    anywhere = pl.BlockSpec(memory_space=pl.ANY)
    vmem = pl.BlockSpec(memory_space=pltpu.VMEM)
    shape = jax.ShapeDtypeStruct((rows_of, width), BF)
    dma = pltpu.SemaphoreType.DMA
    return pl.pallas_call(
        scatter_kernel,
        out_shape=(
            shape, shape, jax.ShapeDtypeStruct((8, rows_of), F32),
            jax.ShapeDtypeStruct((2, piece, hidden), BF),
            jax.ShapeDtypeStruct((2, hidden, piece), BF),
        ),
        in_specs=[anywhere] * 10 + [vmem],
        out_specs=(vmem,) * 5,
        scratch_shapes=[
            pltpu.VMEM((SIDE, 2, 2 * UNIT, width), BF),
            pltpu.VMEM((SIDE, 2, SIDE * rows_of, width), BF),
            pltpu.VMEM((SIDE, 2, 2, half, width), BF),
            pltpu.VMEM((SIDE, 2, 2, rows_of, width), BF),
            pltpu.VMEM((2, 2, half, width), BF),
            pltpu.VMEM((2, 2, rows_of, width), BF),
            pltpu.VMEM((SIDE, 2, 8, 256), F32),
            pltpu.VMEM((SIDE, 2, 8, 256), F32),
            pltpu.VMEM((SIDE, SIDE * 16, rows_of), F32),
            pltpu.VMEM((SIDE, 2, 8, rows_of), F32),
            pltpu.VMEM((SIDE, 2, 16, rows_of), F32),
            pltpu.VMEM((2, 8, rows_of), F32),
            pltpu.VMEM((2, 16, rows_of), F32),
            pltpu.VMEM((REPLICAS, 6, hidden, piece), BF),
            pltpu.VMEM((2, 21, hidden, piece), BF),
            pltpu.VMEM((2, hidden, piece), BF),
            pltpu.VMEM((2, 2, SIDE * rows_of, UNIT), BF),
            dma((SIDE, 2, 3)),
            dma((SIDE, 2, 3)),
            dma((SIDE, 2, 3)),
            dma((SIDE, 3, 2)),
            dma((SIDE, 3, 2)),
            dma((SIDE, 3, 2, 2)),
            dma((SIDE, 3, 2, 2)),
            dma((3, 2)),
            dma((3, 2)),
            dma((3, 2, 2)),
            dma((3, 2, 2)),
            dma((REPLICAS,)),
            dma((2, 21)),
            dma((2, 21)),
            dma((2,)),
            dma((2,)),
            dma((SIDE,)),
            dma((4, SIDE)),
        ],
        compiler_params=pltpu.CompilerParams(
            collective_id=1, has_side_effects=True, vmem_limit_bytes=67043328
        ),
        name="scatter_rows",
    )(*out_rows, *grad_rows, spread, grads, back, kinds, hot_first)


def local(
    tokens,
    cotangent,
    gate_weights,
    expert_ids,
    copy_pick,
    copy_expert,
    up_weight,
    down_weight,
    copy_up,
    copy_down,
):
    me = lax.axis_index("expert")
    rows_of, width = tokens.shape
    table = route(expert_ids.T, copy_pick.T, gate_weights.T, copy_expert)
    *gathered, gates, spread, kinds = gather_rows(tokens, cotangent, table)
    *rows, grads, back = serve(
        copy_expert,
        [part.reshape(-1, width) for part in gathered],
        gates, up_weight, down_weight, copy_up, copy_down,
    )
    rows = [part.reshape(2 * SIDE, -1, width) for part in rows]
    hot_first = copy_expert[(me + 1) % DEVICES] % 2 == 0
    hot_first = jnp.broadcast_to(hot_first.astype(F32), (8, 128))
    results = scatter_rows(
        rows[:3], rows[3:], spread, grads, back, kinds, hot_first, rows_of
    )
    layer_output, token_grad, gate_grad, up_grad, down_grad = finish(*results)
    return layer_output, token_grad, gate_grad.T, up_grad, down_grad


def solution(mesh):
    rows = P(("expert", "dp"), None)
    held = P("expert", None, None)
    return jax.shard_map(
        local,
        mesh=mesh,
        in_specs=(rows,) * 5 + (P(),) + (held,) * 4,
        out_specs=(rows, rows, rows, P("expert", "dp", None), P("expert", None, "dp")),
        check_vma=False,
    )
```

```python
import functools

import jax
import jax.numpy as jnp
from jax import lax
from jax.experimental import pallas as pl
from jax.experimental.pallas import tpu as pltpu
from jax.sharding import PartitionSpec as P

SIDE = 4
HOT, COLD, COPY = 24, 12, 6
SLOTS = 48
REPLICAS = 8
DEVICES = 2 * SIDE * SIDE
HOT_U, COLD_U, COPY_U = SIDE * HOT, SIDE * COLD, 32
UNIT = HOT_U + COLD_U + COPY_U
SPANS = ((0, HOT_U), (HOT_U, COLD_U), (HOT_U + COLD_U, COPY_U))
BF = jnp.bfloat16
F32 = jnp.float32
EXACT = lax.Precision.HIGHEST


def iota(shape, dim):
    return lax.broadcasted_iota(jnp.int32, shape, dim)


def route_kernel(ids_ref, picks_ref, gates_ref, listed_ref, table_ref):
    chosen, rows = ids_ref.shape
    ids, picks, gates = ids_ref[...], picks_ref[...], gates_ref[...]
    devices = listed_ref.shape[0]
    cold = jnp.ones((chosen, rows), jnp.int32)
    for i in range(devices):
        cold = jnp.where(ids == listed_ref[i], 0, cold)
    before = (iota((rows, rows), 0) < iota((rows, rows), 1)).astype(BF)
    lines = iota((128, rows), 0)
    token = iota((128, rows), 1).astype(F32) + 1.0
    offset = jnp.zeros((128, 1), F32)
    table = jnp.zeros((devices, 128), F32)
    for k in range(chosen):
        e, p, g = ids[k : k + 1], picks[k : k + 1], gates[k : k + 1]
        dest = (e // 2 + p) % devices
        region = jnp.where(p == 1, 2, cold[k : k + 1])
        hit = (region * devices + dest == lines).astype(F32)
        ahead = jnp.dot(hit.astype(BF), before, preferred_element_type=F32) + offset
        rank = jnp.sum(hit * ahead, axis=0, keepdims=True).astype(jnp.int32)
        offset = offset + jnp.sum(hit, axis=1, keepdims=True)
        base = jnp.where(region == 0, 0, jnp.where(region == 1, HOT, HOT + COLD))
        slot = base + rank
        to = (dest == iota((devices, rows), 0)).astype(F32)
        code = token + float(k * rows)
        value = jnp.where(slot == lines, code, 0.0) + jnp.where(slot + 64 == lines, g, 0.0)
        table = table + across(to, value, EXACT)
    table_ref[...] = table


def across(a, b, precision=None):
    return lax.dot_general(
        a, b, (((1,), (1,)), ((), ())), precision=precision, preferred_element_type=F32
    )


def route(ids, picks, gates, listed):
    vmem = pl.BlockSpec(memory_space=pltpu.VMEM)
    return pl.pallas_call(
        route_kernel,
        out_shape=jax.ShapeDtypeStruct((listed.shape[0], 128), F32),
        in_specs=[vmem] * 3 + [pl.BlockSpec(memory_space=pltpu.SMEM)],
        out_specs=vmem,
        name="route",
    )(ids, picks, gates, listed)


def seats(s, rows, lead):
    row, lane = iota((rows, 128), 0), iota((rows, 128), 1) - lead
    hot = (row - HOT * s == lane) & (lane >= 0) & (lane < HOT)
    cold = (row - HOT_U - COLD * s == lane - HOT) & (lane >= HOT) & (lane < HOT + COLD)
    copied = (row - HOT_U - COLD_U - COPY * s == lane - HOT - COLD) & (lane >= HOT + COLD)
    copied = copied & (lane < HOT + COLD + COPY)
    return (hot | cold | copied).astype(F32)


def finish_kernel(count, *refs):
    ins, outs, held, sems = refs[:count], refs[count : 2 * count], refs[2 * count : -1], refs[-1]
    loads = [pltpu.make_async_copy(ins[i], held[i], sems.at[0, i]) for i in range(count)]
    stores = [pltpu.make_async_copy(held[i], outs[i], sems.at[1, i]) for i in range(count)]
    for load in loads:
        load.start()
    for load, store in zip(loads, stores):
        load.wait()
        store.start()
    for store in stores:
        store.wait()


def finish(*arrays):
    anywhere = pl.BlockSpec(memory_space=pl.ANY)
    count = len(arrays)
    return pl.pallas_call(
        functools.partial(finish_kernel, count),
        out_shape=tuple(jax.ShapeDtypeStruct(x.shape, x.dtype) for x in arrays),
        in_specs=[anywhere] * count,
        out_specs=(anywhere,) * count,
        scratch_shapes=[pltpu.VMEM(x.shape, x.dtype) for x in arrays]
        + [pltpu.SemaphoreType.DMA((2, count))],
        name="finish",
    )(*arrays)


def serve_kernel(
    which_ref, hot_t, cold_t, copy_t, hot_c, cold_c, copy_c, gates_ref, up_ref, down_ref,
    copy_up_ref, copy_down_ref, hot_o, cold_o, copy_o, hot_g, cold_g, copy_g, grads_ref, back_ref, first_ref,
    x, c, u, v, o, q, w, linear, slope, active, sums, gate_cols, by_unit, in_sem, out_sem,
):
    firsts = (0, hot_t.shape[0], hot_t.shape[0] + cold_t.shape[0])
    counts = (hot_t.shape[0], cold_t.shape[0], copy_t.shape[0])
    width = x.shape[1]
    step = 1024
    me = lax.axis_index("expert")
    hot = which_ref[(me + 1) % DEVICES] % 2
    first_ref[...] = jnp.broadcast_to((1 - hot).astype(F32), first_ref.shape)
    ups = (up_ref.at[hot], up_ref.at[1 - hot], copy_up_ref.at[0])
    downs = (down_ref.at[hot], down_ref.at[1 - hot], copy_down_ref.at[0])

    def loads(r):
        span = pl.ds(firsts[r], counts[r])
        pairs = (
            ((hot_t, cold_t, copy_t)[r], x.at[span]),
            (ups[r], u.at[r]),
            (downs[r], v.at[r]),
            ((hot_c, cold_c, copy_c)[r], c.at[span]),
        )
        return [pltpu.make_async_copy(*pair, in_sem.at[r, i]) for i, pair in enumerate(pairs)]

    stores = []

    def store(src, dst, r, i):
        copy = pltpu.make_async_copy(src, dst, out_sem.at[r, i])
        copy.start()
        stores.append(copy)

    for r in (2, 1, 0):
        for copy in loads(r):
            copy.start()
    for i in range(2 * SIDE):
        columns = jnp.transpose(jnp.broadcast_to(gates_ref[i, :1], (128, gates_ref.shape[2])))
        for r, (low, rows) in enumerate(SPANS):
            gate_cols[pl.ds(firsts[r] + i * rows, rows)] = columns[low : low + rows]
    by_unit[...] = jnp.zeros_like(by_unit)
    for r in (2, 1, 0):
        first, count = firsts[r], counts[r]
        span = pl.ds(first, count)
        ready = loads(r)
        gate = gate_cols[span][:, :1]
        ready[0].wait()
        ready[1].wait()
        tile = count

        @pl.loop(0, count // tile)
        def _(i):
            rows = pl.ds(pl.multiple_of(i * tile, tile), tile)
            value = jnp.dot(
                x[pl.ds(pl.multiple_of(first + i * tile, 128), tile)], u[r],
                preferred_element_type=F32)
            sigma = 1.0 / (1.0 + jnp.exp(-value))
            slope[rows] = sigma * (1.0 + value * (1.0 - sigma))
            active[rows] = (value * sigma).astype(BF)
            linear[rows] = value * sigma

        sums[pl.ds(0, count)] = jnp.zeros((count, 128), F32)
        ready[2].wait()
        ready[3].wait()

        @pl.loop(0, width // step)
        def _(j):
            cols = pl.ds(pl.multiple_of(j * step, step), step)
            served = jnp.dot(
                active[pl.ds(0, count)], v[r, :, cols], preferred_element_type=F32
            )
            cot = c[span, cols].astype(F32)
            both = served * cot
            part = both[:, :128]
            for i in range(1, step // 128):
                part = part + both[:, i * 128 : (i + 1) * 128]
            sums[pl.ds(0, count)] += part
            o[span, cols] = (gate * served).astype(BF)
            c[span, cols] = (gate * cot).astype(BF)

        store(o.at[span], (hot_o, cold_o, copy_o)[r], r, 0)

        @pl.loop(0, count // tile)
        def _(i):
            rows = pl.ds(pl.multiple_of(i * tile, tile), tile)
            value = across(c[pl.ds(pl.multiple_of(first + i * tile, 128), tile)], v[r])
            slope[rows] = value * slope[rows]

        low, rows = SPANS[r]
        totals = jnp.zeros((rows, 128), F32)
        for i in range(2 * SIDE):
            one = jnp.sum(sums[pl.ds(i * rows, rows)], axis=1, keepdims=True)
            totals = jnp.where(iota((rows, 128), 1) == i, one, totals)
        by_unit[pl.ds(low, rows)] = totals
        slanted = slope[pl.ds(0, count)]
        linear_grad = slanted.astype(BF)
        turned = jnp.transpose(slanted).astype(BF)
        active_turned = jnp.transpose(linear[pl.ds(0, count)]).astype(BF)

        @pl.loop(0, width // step)
        def _(j):
            cols = pl.ds(pl.multiple_of(j * step, step), step)
            q[span, cols] = across(linear_grad, u[r, cols]).astype(BF)
            w[r, :, cols] = jnp.dot(turned, x[span, cols], preferred_element_type=F32).astype(BF)
            w[3 + r, :, cols] = jnp.dot(
                active_turned, c[span, cols], preferred_element_type=F32
            ).astype(BF)

        store(q.at[span], (hot_g, cold_g, copy_g)[r], r, 1)
        store(w.at[r], grads_ref.at[r], r, 2)
        store(w.at[3 + r], grads_ref.at[3 + r], r, 3)
    turned = jnp.transpose(by_unit[...])
    for i in range(2 * SIDE):
        back_ref[i] = jnp.broadcast_to(turned[i : i + 1], back_ref.shape[1:])
    for copy in stores:
        copy.wait()


def serve(listed, gathered, gates, up_weight, down_weight, copy_up, copy_down):
    width, hidden = up_weight.shape[1:]
    counts = [rows.shape[0] for rows in gathered[:3]]
    total = sum(counts)
    anywhere = pl.BlockSpec(memory_space=pl.ANY)
    vmem = pl.BlockSpec(memory_space=pltpu.VMEM)
    rows = [jax.ShapeDtypeStruct((count, width), BF) for count in counts]
    return pl.pallas_call(
        serve_kernel,
        out_shape=(
            *rows, *rows, jax.ShapeDtypeStruct((6, hidden, width), BF),
            jax.ShapeDtypeStruct((2 * SIDE, 8, 256), F32), jax.ShapeDtypeStruct((8, 128), F32),
        ),
        in_specs=[pl.BlockSpec(memory_space=pltpu.SMEM)] + [anywhere] * 6 + [vmem] + [anywhere] * 4,
        out_specs=(anywhere,) * 7 + (vmem,) * 2,
        scratch_shapes=[
            pltpu.VMEM((total, width), BF),
            pltpu.VMEM((total, width), BF),
            pltpu.VMEM((3, width, hidden), BF),
            pltpu.VMEM((3, hidden, width), BF),
            pltpu.VMEM((total, width), BF),
            pltpu.VMEM((total, width), BF),
            pltpu.VMEM((6, hidden, width), BF),
            pltpu.VMEM((counts[0], hidden), F32),
            pltpu.VMEM((counts[0], hidden), F32),
            pltpu.VMEM((counts[0], hidden), BF),
            pltpu.VMEM((counts[0], 128), F32),
            pltpu.VMEM((total, 128), F32),
            pltpu.VMEM((256, 128), F32),
            pltpu.SemaphoreType.DMA((3, 4)),
            pltpu.SemaphoreType.DMA((3, 4)),
        ],
        compiler_params=pltpu.CompilerParams(vmem_limit_bytes=62 << 20),
        name="serve",
    )(listed, *gathered, gates, up_weight, down_weight, copy_up, copy_down)


class Place:
    def __init__(self):
        me = lax.axis_index("expert")
        self.me = me
        self.core = me % 2
        x = (me // 2) % SIDE
        y = me // (2 * SIDE)
        self.s = x * (1 - self.core) + y * self.core
        self.b = y * (1 - self.core) + x * self.core

    def at(self, db, ds):
        b = (self.b + db + SIDE) % SIDE
        s = (self.s + ds + SIDE) % SIDE
        y = b * (1 - self.core) + s * self.core
        x = s * (1 - self.core) + b * self.core
        return {"expert": (y * SIDE + x) * 2 + self.core}

    def partner(self):
        return {"expert": self.me + 1 - 2 * self.core}

    def replica(self, dz):
        return {"dp": (lax.axis_index("dp") + dz + REPLICAS) % REPLICAS}

    def before(self):
        return {"expert": (self.me + DEVICES - 1) % DEVICES}

    def beyond(self):
        return {"expert": (self.me + DEVICES - 1 + 2 * self.core) % DEVICES}


def greet(place, *more):
    barrier = pltpu.get_barrier_semaphore()
    others = [place.at(0, 1), place.at(0, -1), place.at(1, 0), place.at(-1, 0), place.partner()]
    others.extend(more)
    for other in others:
        pl.semaphore_signal(barrier, inc=1, device_id=other, device_id_type=pl.DeviceIdType.MESH)
    pl.semaphore_wait(barrier, len(others))


def remote(src, dst, send, recv, device):
    return pltpu.make_async_remote_copy(
        src_ref=src,
        dst_ref=dst,
        send_sem=send,
        recv_sem=recv,
        device_id=device,
        device_id_type=pl.DeviceIdType.MESH,
    )


def gather_kernel(
    tok_ref, cot_ref, table_ref, hot_t, cold_t, copy_t, hot_c, cold_c, copy_c, gates_ref, spread_ref, kinds_ref,
    held, tables, rows, picks, spread, gates, kinds, own_sem, send, recv, out_sem, gate_sem, spread_sem,
):
    place = Place()
    rows_of = tok_ref.shape[0]
    width = tok_ref.shape[1]
    sources = (tok_ref, cot_ref, table_ref)
    outs = ((hot_t, cold_t, copy_t), (hot_c, cold_c, copy_c))
    started = []
    greet(place)

    def start(copy):
        copy.start()
        started.append(copy)
        return copy

    def spot(a, db, ds, part=None):
        b = (place.b + db + SIDE) % SIDE
        s = (place.s + ds + SIDE) % SIDE
        count = sources[a].shape[0]
        half = count // 2
        first = pl.multiple_of(s * count, count)
        within = tables.at[b] if a == 2 else held.at[a, b]
        if part is None:
            return within.at[pl.ds(first, count)]
        return within.at[pl.ds(pl.multiple_of(first + part * half, half), half)]

    def full_s(a, sign):
        return remote(
            sources[a], spot(a, 0, 0), send.at[0, 0, (1 - sign) // 2, a, 0],
            recv.at[0, 0, (1 - sign) // 2, a, 0], place.at(0, sign))

    def half_s(a, sign):
        part = (1 - sign) // 2
        return remote(
            spot(a, 0, -sign, part), spot(a, 0, -sign, part), send.at[1, 0, part, a, 0],
            recv.at[1, 0, part, a, 0], place.at(0, sign))

    def full_b(a, sign, ds):
        src = sources[a] if ds == 0 else spot(a, 0, ds)
        return remote(
            src, spot(a, 0, ds), send.at[0, 1, (1 - sign) // 2, a, ds % SIDE],
            recv.at[0, 1, (1 - sign) // 2, a, ds % SIDE], place.at(sign, 0))

    def half_b(a, sign, ds):
        part = (1 - sign) // 2
        return remote(
            spot(a, -sign, ds, part), spot(a, -sign, ds, part),
            send.at[1, 1, part, a, ds % SIDE], recv.at[1, 1, part, a, ds % SIDE],
            place.at(sign, 0))

    def plan(db):
        b = (place.b + db + SIDE) % SIDE
        slot = db % SIDE
        for h in range(2):
            target = place.me + h * (1 - 2 * place.core)
            scale = jnp.zeros((8, UNIT), F32)
            kind = jnp.zeros((8, UNIT), F32)
            for s in range(SIDE):
                line = tables[b, pl.ds(s * DEVICES + target, 1), :]
                wide = jnp.broadcast_to(line, (128, 128))
                code = wide.astype(jnp.int32) - 1
                token = jnp.where(code >= 0, code % 128, -1)
                one = (jnp.transpose(token.astype(F32)) == iota((128, 128), 1).astype(F32)).astype(BF)
                turned = (token == iota((128, 128), 0)).astype(BF)
                seat = seats(s, UNIT, 0).astype(BF)
                span = pl.ds(s * rows_of, rows_of)
                picks[slot, h, :, span] = jnp.dot(seat, one, preferred_element_type=F32).astype(BF)
                spread[slot, h, span, :] = across(turned, seat).astype(BF)
                scale = scale + across(wide[:8], seats(s, UNIT, 64), EXACT)
                kind = kind + across((code[:8] // 128).astype(F32).astype(BF), seat)
            gates[slot, h, :, pl.ds(0, UNIT)] = scale
            kinds[slot, h, :, pl.ds(0, UNIT)] = kind
        unit = place.core * SIDE + b
        keep(pltpu.make_async_copy(gates.at[slot, 0], gates_ref.at[unit], gate_sem.at[0, slot]))
        start(gates_out(slot))
        keep(pltpu.make_async_copy(spread.at[slot], spread_ref.at[b], spread_sem.at[0, slot]))
        keep(pltpu.make_async_copy(kinds.at[slot], kinds_ref.at[b], spread_sem.at[1, slot]))

    def gates_out(slot):
        b = (place.b + slot) % SIDE
        return remote(
            gates.at[slot, 1], gates_ref.at[place.core * SIDE + b], gate_sem.at[1, slot],
            gate_sem.at[2, slot], place.partner())

    def rows_out(slot, a, r):
        b = (place.b + slot) % SIDE
        first, count = SPANS[r]
        return remote(
            rows.at[slot, a, 1, pl.ds(first, count)], outs[a][r].at[place.core * SIDE + b],
            out_sem.at[1, slot, a, r], out_sem.at[2, slot, a, r], place.partner())

    def pick(db, a):
        b = (place.b + db + SIDE) % SIDE
        slot = db % SIDE
        for h in (1, 0):

            @pl.loop(0, width // 512)
            def _(j):
                cols = pl.ds(pl.multiple_of(j * 512, 512), 512)
                rows[slot, a, h, :, cols] = jnp.dot(
                    picks[slot, h], held[a, b, :, cols], preferred_element_type=F32
                ).astype(BF)

            for r, (first, count) in enumerate(SPANS):
                if h == 1:
                    start(rows_out(slot, a, r))
                else:
                    keep(
                        pltpu.make_async_copy(
                            rows.at[slot, a, 0, pl.ds(first, count)],
                            outs[a][r].at[place.core * SIDE + b], out_sem.at[0, slot, a, r]))

    kept = []

    def keep(copy):
        copy.start()
        kept.append(copy)

    gates[...] = jnp.zeros_like(gates)
    kinds[...] = jnp.zeros_like(kinds)
    arrays = (2, 0, 1)
    for a in arrays:
        for sign in (1, -1):
            start(full_s(a, sign))
        for sign in (1, -1):
            start(full_b(a, sign, 0))
    for a in arrays:
        keep(pltpu.make_async_copy(sources[a], spot(a, 0, 0), own_sem.at[a]))
    for a in arrays:
        for sign in (1, -1):
            full_s(a, sign).wait_recv()
            start(half_s(a, sign))
            for way in (1, -1):
                start(full_b(a, way, -sign))
        for sign in (1, -1):
            full_b(a, sign, 0).wait_recv()
            start(half_b(a, sign, 0))
    for a in arrays:
        for sign in (1, -1):
            half_s(a, sign).wait_recv()
        for way in (1, -1):
            start(full_b(a, way, 2))
    for copy in kept:
        copy.wait()
    kept.clear()
    plan(0)
    for a in range(2):
        pick(0, a)
    for ds in (-1, 1, 2):
        for a in arrays:
            for sign in (1, -1):
                full_b(a, sign, ds).wait_recv()
                start(half_b(a, sign, ds))
    for db in (1, -1):
        plan(db)
        for a in range(2):
            pick(db, a)
    for ds in (0, -1, 1, 2):
        for sign in (1, -1):
            half_b(2, sign, ds).wait_recv()
    plan(2)
    for a in range(2):
        for ds in (0, -1, 1, 2):
            for sign in (1, -1):
                half_b(a, sign, ds).wait_recv()
        pick(2, a)
    for copy in kept:
        copy.wait()
    for slot in range(SIDE):
        gates_out(slot).wait_recv()
        for a in range(2):
            for r in range(3):
                rows_out(slot, a, r).wait_recv()
    for copy in started:
        copy.wait_send()


def gather_rows(tokens, cotangent, table):
    width = tokens.shape[1]
    rows_of = tokens.shape[0]
    shapes = [jax.ShapeDtypeStruct((2 * SIDE, count, width), BF) for _, count in SPANS]
    dma = pltpu.SemaphoreType.DMA
    anywhere = pl.BlockSpec(memory_space=pl.ANY)
    return pl.pallas_call(
        gather_kernel,
        out_shape=(
            *shapes, *shapes, jax.ShapeDtypeStruct((2 * SIDE, 8, 256), F32),
            jax.ShapeDtypeStruct((SIDE, 2, SIDE * rows_of, UNIT), BF),
            jax.ShapeDtypeStruct((SIDE, 2, 8, 256), F32),
        ),
        in_specs=[anywhere] * 3,
        out_specs=(anywhere,) * 9,
        scratch_shapes=[
            pltpu.VMEM((2, SIDE, SIDE * rows_of, width), BF),
            pltpu.VMEM((SIDE, SIDE * DEVICES, 128), F32),
            pltpu.VMEM((SIDE, 2, 2, UNIT, width), BF),
            pltpu.VMEM((SIDE, 2, UNIT, SIDE * rows_of), BF),
            pltpu.VMEM((SIDE, 2, SIDE * rows_of, UNIT), BF),
            pltpu.VMEM((SIDE, 2, 8, 256), F32),
            pltpu.VMEM((SIDE, 2, 8, 256), F32),
            dma((3,)),
            dma((2, 2, 2, 3, SIDE)),
            dma((2, 2, 2, 3, SIDE)),
            dma((3, SIDE, 2, 3)),
            dma((3, SIDE)),
            dma((2, SIDE)),
        ],
        compiler_params=pltpu.CompilerParams(
            collective_id=0, has_side_effects=True, vmem_limit_bytes=60 << 20
        ),
        name="gather_rows",
    )(tokens, cotangent, table)


def scatter_kernel(
    hot_o, cold_o, copy_o, hot_g, cold_g, copy_g, spread_ref, grads_ref, back_ref, kinds_ref, first_ref,
    out_ref, grad_ref, gate_ref, up_ref, down_ref,
    rows, sums, first_in, second_in, third_in, fourth_in,
    backs, kinds, gate_sums, gate_first, gate_second, gate_third, gate_fourth, parts, ring_in, copy_in, spread,
    in_sem, send_r, recv_r, send_1, recv_1, send_2, recv_2, send_3, recv_3, send_4, recv_4,
    part_sem, send_z, recv_z, send_c, recv_c, spread_sem, back_sem,
):
    place = Place()
    width = out_ref.shape[1]
    rows_of = out_ref.shape[0]
    arrays = (2, 0, 1)
    ins = ((hot_o, cold_o, copy_o), (hot_g, cold_g, copy_g))
    order = (2, 3, 1, 0)
    started = []
    greet(place, place.replica(1), place.replica(-1), place.beyond())

    def start(copy):
        copy.start()
        started.append(copy)

    def part_copy(d):
        z = (lax.axis_index("dp") + d) % REPLICAS
        piece = parts.shape[-1]
        return pltpu.make_async_copy(
            grads_ref.at[:, :, pl.ds(pl.multiple_of(z * piece, piece), piece)], parts.at[d],
            part_sem.at[d])

    def ring(sign, k, p):
        way = (1 - sign) // 2
        spot = p % 3 if k == 1 else 6 * k - 9 + p
        return remote(
            parts.at[(sign * (5 - k)) % REPLICAS, p], ring_in.at[way, spot],
            send_z.at[way, spot], recv_z.at[way, spot], place.replica(sign))

    def later(sign):
        return (2, 0, 1) if sign == 1 else (5, 3, 4)

    def ring_start():
        for d in (4, 3, 5, 2, 6, 1, 7, 0):
            part_copy(d).start()
        part_copy(4).wait()
        for i in range(3):
            for sign in (1, -1):
                start(ring(sign, 1, later(sign)[i]))
        part_copy(3).wait()
        part_copy(5).wait()
        for i in range(3):
            for sign in (1, -1):
                start(ring(sign, 2, later(-sign)[i]))
        for d in (2, 6, 1, 7, 0):
            part_copy(d).wait()

    def ring_step(k, second):
        for i in range(3):
            for sign in (1, -1):
                p = later(sign if second else -sign)[i]
                ring(sign, k, p).wait_recv()
                spot = p % 3 if k == 1 else 6 * k - 9 + p
                add(parts.at[(sign * (4 - k)) % REPLICAS, p], ring_in.at[(1 - sign) // 2, spot])
                start(ring(sign, k + 1, p))

    def hand_over(i):
        return remote(
            parts.at[0, 3 * i + 2], copy_in.at[i], send_c.at[i], recv_c.at[i], place.before())

    def ring_end(p):
        for sign in (1, -1):
            ring(sign, 4, p).wait_recv()
        spot = 15 + p
        if p % 3 == 2:
            add(parts.at[0, p], ring_in.at[0, spot], ring_in.at[1, spot])
            start(hand_over(p // 3))
            return None
        total = parts[0, p].astype(F32)
        for way in range(2):
            total = total + ring_in[way, spot].astype(F32)
        if p % 3 == 0:
            hand_over(p // 3).wait_recv()
            total = total + copy_in[p // 3].astype(F32)
        return total

    def ring_result(i, result):
        cold = ring_end(3 * i + 1)
        hot = ring_end(3 * i)
        hot_first = first_ref[:1, :1] > 0.5
        for e, value in enumerate((jnp.where(hot_first, hot, cold), jnp.where(hot_first, cold, hot))):
            result[e] = (jnp.transpose(value) if i == 0 else value).astype(BF)

    def unit_copies(slot, a, r):
        first, count = SPANS[r]
        b = (place.b + slot) % SIDE
        return pltpu.make_async_copy(
            ins[a][r].at[place.core * SIDE + b], rows.at[slot, a, pl.ds(first, count)],
            in_sem.at[slot, a, r])

    def unit_sends(slot, a, r):
        first, count = SPANS[r]
        b = (place.s + slot) % SIDE
        return remote(
            ins[a][r].at[(1 - place.core) * SIDE + b],
            rows.at[slot, a, pl.ds(UNIT + first, count)],
            send_r.at[slot, a, r], recv_r.at[slot, a, r], place.partner())

    def chunk(slot, a, ds, part=None):
        s = (place.s + ds + SIDE) % SIDE
        count = 16 if a == 2 else rows_of
        within = gate_sums.at[slot] if a == 2 else sums.at[slot, a]
        first = pl.multiple_of(s * count, count)
        if part is None:
            return within.at[pl.ds(first, count)]
        half = count // 2
        return within.at[pl.ds(pl.multiple_of(first + part * half, half), half)]

    def half_of(within, part):
        half = within.shape[0] // 2
        return within.at[pl.ds(part * half, half)]

    def first_at(slot, a, part):
        return gate_first.at[slot, part] if a == 2 else first_in.at[slot, a, part]

    def second_at(slot, a, way):
        return gate_second.at[slot, way] if a == 2 else second_in.at[slot, a, way]

    def third_at(a, part):
        return gate_third.at[part] if a == 2 else third_in.at[a, part]

    def fourth_at(a, way):
        return gate_fourth.at[way] if a == 2 else fourth_in.at[a, way]

    def far(slot, a, sign):
        part = (1 - sign) // 2
        return remote(
            chunk(slot, a, 2, part), first_at(slot, a, part),
            send_1.at[slot, a, part], recv_1.at[slot, a, part], place.at(0, sign))

    def near(slot, a, sign, part):
        way = (1 - sign) // 2
        return remote(
            chunk(slot, a, sign, part), half_of(second_at(slot, a, way), part),
            send_2.at[slot, a, way, part], recv_2.at[slot, a, way, part],
            place.at(0, sign))

    def far_b(a, sign):
        part = (1 - sign) // 2
        return remote(
            chunk(2, a, 0, part), third_at(a, part),
            send_3.at[a, part], recv_3.at[a, part], place.at(sign, 0))

    def near_b(a, sign, part):
        way = (1 - sign) // 2
        return remote(
            chunk(sign % SIDE, a, 0, part), half_of(fourth_at(a, way), part),
            send_4.at[a, way, part], recv_4.at[a, way, part], place.at(sign, 0))

    def add(into, *others):
        step = min(32, into.shape[0])

        @pl.loop(0, into.shape[0] // step)
        def _(i):
            span = pl.ds(pl.multiple_of(i * step, step), step)
            total = into[span].astype(F32)
            for other in others:
                total = total + other[span].astype(F32)
            into[span] = total.astype(into.dtype)

    def back_copies(slot):
        b = (place.b + slot) % SIDE
        return (
            pltpu.make_async_copy(
                back_ref.at[place.core * SIDE + b], backs.at[slot, 0], back_sem.at[0, slot]),
            pltpu.make_async_copy(kinds_ref.at[b], kinds.at[slot], back_sem.at[1, slot]),
        )

    def back_send(slot):
        b = (place.s + slot) % SIDE
        return remote(
            back_ref.at[(1 - place.core) * SIDE + b], backs.at[slot, 1],
            back_sem.at[2, slot], back_sem.at[3, slot], place.partner())

    for slot in order:
        start(back_send(slot))
        for copy in back_copies(slot):
            copy.start()
        for a in range(2):
            for r in range(3):
                start(unit_sends(slot, a, r))
                unit_copies(slot, a, r).start()

    def spread_copy(slot):
        b = (place.b + slot) % SIDE
        turn = order.index(slot) % 2
        return pltpu.make_async_copy(spread_ref.at[b], spread.at[turn], spread_sem.at[slot])

    for slot in order[:2]:
        spread_copy(slot).start()

    def expand(slot):
        turn = order.index(slot)
        spread_copy(slot).wait()
        for copy in back_copies(slot):
            copy.wait()
        back_send(slot).wait_recv()
        gate = jnp.zeros((8, SIDE * rows_of), F32)
        for h in range(2):
            kind = kinds[slot, h, :, pl.ds(0, UNIT)]
            rest = backs[slot, h, :, pl.ds(0, UNIT)]
            rest = jnp.where(kind == iota((8, UNIT), 0).astype(F32), rest, 0.0)
            for _ in range(3):
                top = rest.astype(BF)
                rest = rest - top.astype(F32)
                gate = gate + across(top, spread[turn % 2, h])
        for s in range(SIDE):
            gate_sums[slot, pl.ds(16 * s, 8)] = gate[:, s * rows_of : (s + 1) * rows_of]
            gate_sums[slot, pl.ds(16 * s + 8, 8)] = jnp.zeros((8, rows_of), F32)
        for sign in (1, -1):
            start(far(slot, 2, sign))
        for sign in (1, -1):
            start(near(slot, 2, sign, (1 + sign) // 2))
        for a in range(2):
            for r in range(3):
                unit_copies(slot, a, r).wait()
                unit_sends(slot, a, r).wait_recv()

            @pl.loop(0, width // 512)
            def _(j):
                cols = pl.ds(pl.multiple_of(j * 512, 512), 512)
                own = jnp.dot(
                    spread[turn % 2, 0], rows[slot, a, pl.ds(0, UNIT), cols],
                    preferred_element_type=F32)
                other = jnp.dot(
                    spread[turn % 2, 1], rows[slot, a, pl.ds(UNIT, UNIT), cols],
                    preferred_element_type=F32)
                sums[slot, a, :, cols] = (own + other).astype(BF)

            for sign in (1, -1):
                start(far(slot, a, sign))
            for sign in (1, -1):
                start(near(slot, a, sign, (1 + sign) // 2))
        if turn < 2:
            spread_copy(order[turn + 2]).start()

    def pass_on(slot):
        for a in arrays:
            for sign in (1, -1):
                part = (1 - sign) // 2
                far(slot, a, sign).wait_recv()
                add(chunk(slot, a, sign, part), first_at(slot, a, part))
                start(near(slot, a, sign, part))

    def finish(slot):
        for a in arrays:
            for sign in (1, -1):
                for part in range(2):
                    near(slot, a, sign, part).wait_recv()
            add(chunk(slot, a, 0), second_at(slot, a, 0), second_at(slot, a, 1))

    ring_start()
    expand(2)
    expand(3)
    pass_on(2)
    ring_step(1, True)
    expand(1)
    ring_step(2, False)
    pass_on(3)
    finish(2)
    for a in arrays:
        for sign in (1, -1):
            start(far_b(a, sign))
    expand(0)
    ring_step(2, True)
    pass_on(1)
    finish(3)
    for a in arrays:
        start(near_b(a, -1, 0))
    ring_step(3, False)
    pass_on(0)
    finish(1)
    for a in arrays:
        start(near_b(a, 1, 1))
    ring_step(3, True)
    for a in arrays:
        for sign in (1, -1):
            part = (1 - sign) // 2
            far_b(a, sign).wait_recv()
            add(chunk(sign % SIDE, a, 0, part), third_at(a, part))
            start(near_b(a, sign, part))
    finish(0)
    for p in (5, 2):
        ring_end(p)
    for a in arrays:
        for sign in (1, -1):
            for part in range(2):
                near_b(a, sign, part).wait_recv()
        add(chunk(0, a, 0), fourth_at(a, 0), fourth_at(a, 1))
        if a == 2:
            gate_ref[...] = chunk(0, a, 0, 0)[...]
        else:
            (out_ref, grad_ref)[a][...] = chunk(0, a, 0)[...]
    ring_result(1, down_ref)
    ring_result(0, up_ref)
    for copy in started:
        copy.wait_send()


def scatter_rows(out_rows, grad_rows, spread, grads, back, kinds, hot_first, rows_of):
    width = out_rows[0].shape[-1]
    hidden = grads.shape[1]
    piece = width // REPLICAS
    half = rows_of // 2
    anywhere = pl.BlockSpec(memory_space=pl.ANY)
    vmem = pl.BlockSpec(memory_space=pltpu.VMEM)
    shape = jax.ShapeDtypeStruct((rows_of, width), BF)
    dma = pltpu.SemaphoreType.DMA
    return pl.pallas_call(
        scatter_kernel,
        out_shape=(
            shape, shape, jax.ShapeDtypeStruct((8, rows_of), F32),
            jax.ShapeDtypeStruct((2, piece, hidden), BF),
            jax.ShapeDtypeStruct((2, hidden, piece), BF),
        ),
        in_specs=[anywhere] * 10 + [vmem],
        out_specs=(vmem,) * 5,
        scratch_shapes=[
            pltpu.VMEM((SIDE, 2, 2 * UNIT, width), BF),
            pltpu.VMEM((SIDE, 2, SIDE * rows_of, width), BF),
            pltpu.VMEM((SIDE, 2, 2, half, width), BF),
            pltpu.VMEM((SIDE, 2, 2, rows_of, width), BF),
            pltpu.VMEM((2, 2, half, width), BF),
            pltpu.VMEM((2, 2, rows_of, width), BF),
            pltpu.VMEM((SIDE, 2, 8, 256), F32),
            pltpu.VMEM((SIDE, 2, 8, 256), F32),
            pltpu.VMEM((SIDE, SIDE * 16, rows_of), F32),
            pltpu.VMEM((SIDE, 2, 8, rows_of), F32),
            pltpu.VMEM((SIDE, 2, 16, rows_of), F32),
            pltpu.VMEM((2, 8, rows_of), F32),
            pltpu.VMEM((2, 16, rows_of), F32),
            pltpu.VMEM((REPLICAS, 6, hidden, piece), BF),
            pltpu.VMEM((2, 21, hidden, piece), BF),
            pltpu.VMEM((2, hidden, piece), BF),
            pltpu.VMEM((2, 2, SIDE * rows_of, UNIT), BF),
            dma((SIDE, 2, 3)),
            dma((SIDE, 2, 3)),
            dma((SIDE, 2, 3)),
            dma((SIDE, 3, 2)),
            dma((SIDE, 3, 2)),
            dma((SIDE, 3, 2, 2)),
            dma((SIDE, 3, 2, 2)),
            dma((3, 2)),
            dma((3, 2)),
            dma((3, 2, 2)),
            dma((3, 2, 2)),
            dma((REPLICAS,)),
            dma((2, 21)),
            dma((2, 21)),
            dma((2,)),
            dma((2,)),
            dma((SIDE,)),
            dma((4, SIDE)),
        ],
        compiler_params=pltpu.CompilerParams(
            collective_id=1, has_side_effects=True, vmem_limit_bytes=67043328
        ),
        name="scatter_rows",
    )(*out_rows, *grad_rows, spread, grads, back, kinds, hot_first)


def local(
    tokens,
    cotangent,
    gate_weights,
    expert_ids,
    copy_pick,
    copy_expert,
    up_weight,
    down_weight,
    copy_up,
    copy_down,
):
    rows_of, width = tokens.shape
    table = route(expert_ids.T, copy_pick.T, gate_weights.T, copy_expert)
    *gathered, gates, spread, kinds = gather_rows(tokens, cotangent, table)
    *rows, grads, back, hot_first = serve(
        copy_expert,
        [part.reshape(-1, width) for part in gathered],
        gates, up_weight, down_weight, copy_up, copy_down,
    )
    rows = [part.reshape(2 * SIDE, -1, width) for part in rows]
    results = scatter_rows(
        rows[:3], rows[3:], spread, grads, back, kinds, hot_first, rows_of
    )
    layer_output, token_grad, gate_grad, up_grad, down_grad = finish(*results)
    return layer_output, token_grad, gate_grad.T, up_grad, down_grad


def solution(mesh):
    rows = P(("expert", "dp"), None)
    held = P("expert", None, None)
    return jax.shard_map(
        local,
        mesh=mesh,
        in_specs=(rows,) * 5 + (P(),) + (held,) * 4,
        out_specs=(rows, rows, rows, P("expert", "dp", None), P("expert", None, "dp")),
        check_vma=False,
    )
```
